32 devices in a mesh: cuts: 2 (over x), tile: 16 (over z, y, core).
Axes of the slice: x: 2, y: 2, z: 4, core: 2. Of those that a mesh axis runs over, the one named last changes fastest.
Arguments:
- object_delta: float32 [2, 2, 2048, 4096], P('cuts', None, None, 'tile'), may hold values from -1.2 to 1.2
- probe_wave: bfloat16 [2, 256, 256], replicated, may hold values from -4 to 4
- intensity: float32 [32, 256, 256], P('tile'), may hold values from 0 to 2
- positions: int32 [32, 2], P('tile'), may hold values from 0 to 3840, as said below
Outputs:
- object_gradient: float32 [2, 2, 2048, 4096], P('cuts', None, None, 'tile')
The draws below stay inside these ranges and needn't reach their ends.
Inputs may be any that keep to these rules, and one draw needn't show every extreme that they name: `positions`: row entries run from 0 to 1792. The column of probe k lies in columns (k // 2) * 256 to (k // 2) * 256 + 255, and equals (k // 2) * 256 for the probes of the last block of 2.
All inputs are finite; a program needn't handle non-finite values.
Results may differ from the reference program's by a relative error of at most 0.04.
Values may be sent and summed in bfloat16 or wider, within the bound.
A program may use at most 64 MiB of HBM per device.

```python
import math
import jax
import jax.numpy as jnp
from jax import lax

PROBE = 256
PR_DEV = 2
OBJ_ROWS = 2048
TILE_COLS = 256
SLICES = 2
PROBES = 32
OBJ_COLS = 4096


def draw_positions(key, part):
    row_key = jax.random.fold_in(key, 101)
    column_key = jax.random.fold_in(key, 202)
    corner_rows = jax.random.randint(row_key, (PROBES,), 0, OBJ_ROWS - PROBE + 1, dtype=jnp.int32)
    corner_rows = corner_rows.at[0].set(0).at[PROBES - 1].set(OBJ_ROWS - PROBE)
    owner_tile = jnp.arange(PROBES, dtype=jnp.int32) // PR_DEV
    offset = jax.random.randint(column_key, (PROBES,), 0, TILE_COLS, dtype=jnp.int32)
    offset = jnp.where(owner_tile == PROBES // PR_DEV - 1, 0, offset)
    corner_cols = owner_tile * TILE_COLS + offset
    return jnp.stack([corner_rows, corner_cols], axis=1).astype(jnp.int32)


def block_scale(rng, extent, shards, low, largest):
    level, own = 1.0, jax.random.fold_in(rng, 6)
    for dim, shards_of in shards:
        steps = jnp.exp(jax.random.uniform(jax.random.fold_in(own, dim), (shards_of,), jnp.float32, low / len(shards), largest / len(shards)))
        level = level * jnp.repeat(steps, extent[dim] // shards_of).reshape([-1 if axis == dim else 1 for axis in range(len(extent))])
    return level


def centred(rng, dims, spread, reach, pieces=(), kind=jnp.bfloat16):
    gain = block_scale(rng, dims, pieces, -0.22, 0.18) if pieces else 1.0
    entries = jax.random.normal(rng, dims, jnp.float32) * spread * gain
    return jnp.minimum(jnp.maximum(entries, -reach), reach).astype(kind)


def setup_inputs(seed: int = 0) -> dict:
    streams_of = jax.random.split(jax.random.key(seed), 5)
    object_delta = centred(streams_of[0], (SLICES, 2, OBJ_ROWS, OBJ_COLS), 0.2, 1.2, ((0, 2), (3, 16)), jnp.float32)
    probe_wave = centred(streams_of[1], (2, PROBE, PROBE), 0.6, 4.0)
    intensity = jnp.clip(2.0 * jax.random.uniform(streams_of[2], (PROBES, PROBE, PROBE), jnp.float32) ** block_scale(streams_of[2], (PROBES, PROBE, PROBE), ((0, 16),), -0.2, 0.2), 0.0, 2.0)
    positions = draw_positions(jax.random.fold_in(streams_of[4], 71), 0)
    return {"object_delta": object_delta, "probe_wave": probe_wave, "intensity": intensity, "positions": positions}


HIGHEST = lax.Precision.HIGHEST

def make_tables(probe_width):
    counter = jnp.arange(probe_width, dtype=jnp.int32)
    phase_table = (counter[:, None] * counter[None, :] % probe_width).astype(jnp.float32) * (2.0 * math.pi / probe_width)
    norm_scale = 1.0 / math.sqrt(probe_width)
    four_re = jnp.cos(phase_table) * norm_scale
    four_im = -jnp.sin(phase_table) * norm_scale
    signed = jnp.where(counter < probe_width // 2, counter, counter - probe_width).astype(jnp.float32)
    kernel_phase = -2.0 * math.pi / probe_width * signed * signed
    kernel_re = jnp.cos(kernel_phase)[:, None]
    kernel_im = jnp.sin(kernel_phase)[:, None]
    scaled_re = kernel_re * four_re - kernel_im * four_im
    scaled_im = kernel_re * four_im + kernel_im * four_re
    prop_re = (jnp.dot(four_re, scaled_re, precision=HIGHEST) + jnp.dot(four_im, scaled_im, precision=HIGHEST)).astype(jnp.bfloat16)
    prop_im = (jnp.dot(four_re, scaled_im, precision=HIGHEST) - jnp.dot(four_im, scaled_re, precision=HIGHEST)).astype(jnp.bfloat16)
    four_re = four_re.astype(jnp.bfloat16)
    four_im = four_im.astype(jnp.bfloat16)
    far_forward = ((four_re, four_im), (four_re, four_im))
    far_adjoint = ((four_re, -four_im), (four_re, -four_im))
    prop_forward = ((prop_re, prop_im), (prop_re.T, prop_im.T))
    prop_adjoint = ((prop_re.T, -prop_im.T), (prop_re, -prop_im))
    return (far_forward, far_adjoint, prop_forward, prop_adjoint)

def complex_dot(left_re, left_im, right_re, right_im):
    real_part = jnp.dot(left_re, right_re, preferred_element_type=jnp.float32) - jnp.dot(left_im, right_im, preferred_element_type=jnp.float32)
    imag_part = jnp.dot(left_re, right_im, preferred_element_type=jnp.float32) + jnp.dot(left_im, right_re, preferred_element_type=jnp.float32)
    return (real_part, imag_part)

def sandwich(wave_re, wave_im, operands):
    (left_re, left_im), (right_re, right_im) = operands
    inner_re, inner_im = complex_dot(left_re, left_im, wave_re, wave_im)
    return complex_dot(inner_re.astype(jnp.bfloat16), inner_im.astype(jnp.bfloat16), right_re, right_im)

def probe_gradient(object_delta, probe_wave, intensity_one, corner_row, corner_col, tables):
    far_forward, far_adjoint, prop_forward, prop_adjoint = tables
    anchor = jnp.zeros((), jnp.int32)
    patches = lax.dynamic_slice(object_delta, (anchor, anchor, corner_row, corner_col), (object_delta.shape[0], 2, PROBE, PROBE))

    def forward_step(wave_in, patch_now):
        trans_re = 1.0 + patch_now[0]
        trans_im = patch_now[1]
        wave_re = wave_in[0].astype(jnp.float32)
        wave_im = wave_in[1].astype(jnp.float32)
        exit_re = wave_re * trans_re - wave_im * trans_im
        exit_im = wave_re * trans_im + wave_im * trans_re
        out_re, out_im = sandwich(exit_re.astype(jnp.bfloat16), exit_im.astype(jnp.bfloat16), prop_forward)
        return (jnp.stack([out_re, out_im]).astype(jnp.bfloat16), wave_in)
    final_wave, stored = lax.scan(forward_step, probe_wave, patches)
    far_re, far_im = sandwich(final_wave[0], final_wave[1], far_forward)
    misfit = far_re * far_re + far_im * far_im - intensity_one
    seed_re, seed_im = sandwich((misfit * far_re).astype(jnp.bfloat16), (misfit * far_im).astype(jnp.bfloat16), far_adjoint)
    seed_wave = jnp.stack([seed_re, seed_im]).astype(jnp.bfloat16)

    def adjoint_step(adjoint_in, scan_pair):
        stored_now, patch_now = scan_pair
        back_re, back_im = sandwich(adjoint_in[0], adjoint_in[1], prop_adjoint)
        wave_re = stored_now[0].astype(jnp.float32)
        wave_im = stored_now[1].astype(jnp.float32)
        grad_re = wave_re * back_re + wave_im * back_im
        grad_im = wave_re * back_im - wave_im * back_re
        trans_re = 1.0 + patch_now[0]
        trans_im = patch_now[1]
        new_re = trans_re * back_re + trans_im * back_im
        new_im = trans_re * back_im - trans_im * back_re
        return (jnp.stack([new_re, new_im]).astype(jnp.bfloat16), jnp.stack([grad_re, grad_im]))
    _, gradients = lax.scan(adjoint_step, seed_wave, (stored, patches), reverse=True)
    return gradients

def reference(object_delta, probe_wave, intensity, positions):
    tables = make_tables(PROBE)
    initial = jnp.zeros(object_delta.shape, jnp.float32)

    def accumulate(running, scan_item):
        intensity_one, corner = scan_item
        corner_row = corner[0]
        corner_col = corner[1]
        gradients = probe_gradient(object_delta, probe_wave, intensity_one, corner_row, corner_col, tables)
        anchor = jnp.zeros((), jnp.int32)
        start_at = (anchor, anchor, corner_row, corner_col)
        previous = lax.dynamic_slice(running, start_at, gradients.shape)
        return (lax.dynamic_update_slice(running, previous + gradients, start_at), None)
    result, _ = lax.scan(accumulate, initial, (intensity, positions))
    return result
```

```python
import functools
import math

import jax
import jax.numpy as jnp
import numpy as np
from jax import lax
from jax.experimental import pallas as pl
from jax.experimental.pallas import tpu as pltpu
from jax.sharding import PartitionSpec as P

F32 = jnp.float32
BF16 = jnp.bfloat16
MESH = pl.DeviceIdType.MESH
LANE_ROWS = 8


def make_tables(width):
    counter = np.arange(width)
    phase = (counter[:, None] * counter[None, :] % width) * (2.0 * math.pi / width)
    four = np.exp(-1j * phase) / math.sqrt(width)
    signed = np.where(counter < width // 2, counter, counter - width).astype(np.float64)
    kernel = np.exp(-2j * math.pi / width * signed * signed)
    prop = np.conj(four) @ (kernel[:, None] * four)
    prop = 0.5 * (prop + prop.T)

    def block(table):
        re, im = table.real, table.imag
        return np.block([[re, -im], [im, re]])

    big = [block(prop), block(prop).T, block(four), block(four).T]
    return np.stack(big).astype(np.float32).astype(jnp.bfloat16)


def dot(a, b):
    return jnp.dot(a, b, preferred_element_type=F32)


def repeat(count, body):
    if count == 1:
        body(0)
    elif count > 1:
        lax.fori_loop(0, count, lambda i, _: (body(i), 0)[1], 0)


def exchange_kernel(
    obj_hbm, probe_hbm, inten_hbm, pos, tabs_hbm,
    own_out, strip_out, left_out,
    obj_v, probe_v, inten_v, tabs_v, strip_send, strip_recv, win, psi, lam, grad_send,
    obj_sem, load_sem, pos_sem, strip_ssem, strip_rsem, x_ssem, x_rsem, g_ssem, g_rsem,
    *, chunks, gchunks,
):
    cut, tile = lax.axis_index("cuts"), lax.axis_index("tile")
    ncut, ntile = lax.axis_size("cuts"), lax.axis_size("tile")
    per, cols = obj_v.shape[0], obj_v.shape[-1]
    groups = obj_hbm.shape[2]
    count, width = inten_v.shape[0], inten_v.shape[1]
    total = ncut * per
    height = width // chunks
    gheight = width // gchunks
    has_left, has_right = tile > 0, tile < ntile - 1
    left, right = {"tile": tile - 1}, {"tile": tile + 1}

    loads = obj_sem.shape[-1]
    load_groups = groups // loads

    def obj_copy(j, part, q):
        span = pl.ds(q * load_groups, load_groups)
        return pltpu.make_async_copy(
            obj_hbm.at[j, part, span], obj_v.at[j, part, span], obj_sem.at[j, part, q]
        )

    probe_copy = pltpu.make_async_copy(probe_hbm, probe_v, load_sem.at[1])
    tabs_copy = pltpu.make_async_copy(tabs_hbm, tabs_v, load_sem.at[2])
    inten_copy = pltpu.make_async_copy(inten_hbm, inten_v, load_sem.at[3])
    for j in range(per):
        for part in range(2):
            for q in range(loads):
                obj_copy(j, part, q).start()
    probe_copy.start()

    barrier = pltpu.get_barrier_semaphore()

    @pl.when(has_left)
    def _():
        pl.semaphore_signal(barrier, inc=1, device_id=left, device_id_type=MESH)

    @pl.when(has_right)
    def _():
        pl.semaphore_signal(barrier, inc=1, device_id=right, device_id_type=MESH)

    for o in range(1, ncut):
        peer = {"cuts": lax.rem(cut + o, ncut)}
        pl.semaphore_signal(barrier, inc=1, device_id=peer, device_id_type=MESH)
    peers = ncut - 1 + jnp.where(has_left, 1, 0) + jnp.where(has_right, 1, 0)
    pl.semaphore_wait(barrier, peers)

    pos_copy = pltpu.make_async_remote_copy(
        src_ref=pos, dst_ref=left_out, send_sem=pos_sem.at[0], recv_sem=pos_sem.at[1],
        device_id=right, device_id_type=MESH,
    )

    @pl.when(has_right)
    def _():
        pos_copy.start()

    lanes = lax.broadcasted_iota(jnp.int32, (height, cols), 1)
    glanes = lax.broadcasted_iota(jnp.int32, (gheight, cols), 1)
    first_lines = lax.broadcasted_iota(jnp.int32, (LANE_ROWS, cols), 0)

    def window_rows(row, j, part, k):
        base = lax.div(row, LANE_ROWS)
        part_groups = height // LANE_ROWS
        main = obj_v[j, part, pl.ds(base + k * part_groups, part_groups)].reshape(height, cols)
        if k > 0:
            return main
        wrapped = obj_v[j, part, base + width // LANE_ROWS]
        head = jnp.where(first_lines < row - base * LANE_ROWS, wrapped, main[:LANE_ROWS])
        return jnp.concatenate([head, main[LANE_ROWS:]], axis=0)

    def strip_copy(p, k):
        span = pl.ds(k * height, height)
        return pltpu.make_async_remote_copy(
            src_ref=strip_send.at[p, :, :, span, :], dst_ref=strip_recv.at[p, :, :, span, :],
            send_sem=strip_ssem.at[p, k], recv_sem=strip_rsem.at[p, k],
            device_id=left, device_id_type=MESH,
        )

    def cross_copy(o, source, p, k):
        span = pl.ds(k * height, height)
        part = win.at[p, source, :, :, span, :]
        return pltpu.make_async_remote_copy(
            src_ref=part, dst_ref=part,
            send_sem=x_ssem.at[o - 1, p, k], recv_sem=x_rsem.at[o - 1, p, k],
            device_id={"cuts": lax.rem(cut + o, ncut)}, device_id_type=MESH,
        )

    def grad_copy(p, k):
        span = pl.ds(k * gheight, gheight)
        return pltpu.make_async_remote_copy(
            src_ref=grad_send.at[p, :, :, span, :], dst_ref=strip_out.at[p, :, :, span, :],
            send_sem=g_ssem.at[p, k], recv_sem=g_rsem.at[p, k],
            device_id=right, device_id_type=MESH,
        )

    for j in range(per):
        for part in range(2):
            for q in range(loads):
                obj_copy(j, part, q).wait()

            obj_v[j, part, groups] = jnp.zeros((LANE_ROWS, cols), F32)

    tabs_copy.start()
    inten_copy.start()

    @pl.when(has_left)
    def _():
        pos_copy.wait_recv()
        for p in range(count):
            for k in range(chunks):
                for j in range(per):
                    for part in range(2):
                        strip_send[p, j, part, k * height : (k + 1) * height] = window_rows(
                            left_out[p, 0], j, part, k
                        ).astype(BF16)
                strip_copy(p, k).start()

    @pl.when(jnp.logical_not(has_left))
    def _():
        for p in range(count):
            for d in range(2):
                left_out[p, d] = 0
        strip_out[...] = jnp.zeros_like(strip_out)

    @pl.when(jnp.logical_not(has_right))
    def _():
        strip_recv[...] = jnp.zeros_like(strip_recv)

    for p in range(count):
        col = pos[p, 1] - tile * cols
        for k in range(chunks):

            @pl.when(has_right)
            def _():
                strip_copy(p, k).wait_recv()

            span = pl.ds(k * height, height)
            for j in range(per):
                for part in range(2):
                    win[p, cut, j, part, span, :] = jnp.where(
                        lanes >= col,
                        window_rows(pos[p, 0], j, part, k),
                        strip_recv[p, j, part, span, :].astype(F32),
                    ).astype(BF16)
            for o in range(1, ncut):
                cross_copy(o, cut, p, k).start()

    probe_copy.wait()
    across = lax.broadcasted_iota(jnp.int32, (width, width), 1)
    down = lax.broadcasted_iota(jnp.int32, (width, width), 0)
    for p in range(count):
        row, col = pos[p, 0], pos[p, 1] - tile * cols
        shift = row - row // LANE_ROWS * LANE_ROWS
        source = across + shift
        move_rows = jnp.where(jnp.where(source >= width, source - width, source) == down, 1.0, 0.0)
        source = down + col
        move_cols = jnp.where(jnp.where(source >= width, source - width, source) == across, 1.0, 0.0)
        for part in range(2):
            moved = dot(move_rows.astype(BF16), probe_v[part]).astype(BF16)
            psi[p, 0, part] = dot(moved, move_cols.astype(BF16)).astype(BF16)

    tabs_copy.wait()
    inten_copy.wait()

    def arrive(p, owner):
        @pl.when(owner != cut)
        def _():
            o = lax.rem(cut - owner + ncut, ncut)
            for k in range(chunks):
                cross_copy(o, owner, p, k).wait_recv()

    def sandwich(first, second, stacked):
        inner = dot(tabs_v[first], stacked).astype(BF16)
        side = jnp.concatenate([inner[:width], inner[width:]], axis=1)
        return dot(side, tabs_v[second])

    def exit_wave(p, s):
        owner, j = s // per, lax.rem(s, per)
        t_re = 1.0 + win[p, owner, j, 0].astype(F32)
        t_im = win[p, owner, j, 1].astype(F32)
        p_re, p_im = psi[p, s, 0].astype(F32), psi[p, s, 1].astype(F32)
        x_re = (p_re * t_re - p_im * t_im).astype(BF16)
        x_im = (p_re * t_im + p_im * t_re).astype(BF16)
        return jnp.concatenate([x_re, x_im], axis=0)

    def adjoint_slice(p, s, first, second, stacked):
        owner, j = s // per, lax.rem(s, per)
        col = pos[p, 1] - tile * cols
        inner = dot(tabs_v[first], stacked).astype(BF16)
        side = jnp.concatenate([inner[:width], inner[width:]], axis=1)

        @pl.when(owner == cut)
        def _():
            for k in range(gchunks):
                span = pl.ds(k * gheight, gheight)
                mu = dot(side[k * gheight : (k + 1) * gheight], tabs_v[second])
                m_re, m_im = mu[:, :width], mu[:, width:]
                p_re = psi[p, s, 0, span, :].astype(F32)
                p_im = psi[p, s, 1, span, :].astype(F32)
                g = (p_re * m_re + p_im * m_im, p_re * m_im - p_im * m_re)
                for part in range(2):
                    own_out[p, j, part, span, :] = jnp.where(glanes >= col, g[part], 0.0)
                    grad_send[p, j, part, span, :] = jnp.where(glanes >= col, 0.0, g[part]).astype(
                        BF16
                    )
                if per == 1:

                    @pl.when(has_right)
                    def _():
                        grad_copy(p, k).start()

        @pl.when(s > cut * per)
        def _():
            mu = dot(side, tabs_v[second])
            m_re, m_im = mu[:, :width], mu[:, width:]
            t_re = 1.0 + win[p, owner, j, 0].astype(F32)
            t_im = win[p, owner, j, 1].astype(F32)
            lam[:width] = (t_re * m_re + t_im * m_im).astype(BF16)
            lam[width:] = (t_re * m_im - t_im * m_re).astype(BF16)

    def one_probe(p):
        def forward(s):
            arrive(p, s // per)
            out = sandwich(0, 1, exit_wave(p, s))
            psi[p, s + 1, 0] = out[:, :width].astype(BF16)
            psi[p, s + 1, 1] = out[:, width:].astype(BF16)

        def backward(i):
            s = total - 2 - i

            @pl.when(s >= cut * per)
            def _():
                adjoint_slice(p, s, 1, 0, lam[...])

        if per == 1:
            repeat(total - 1, forward)
            arrive(p, total - 1)
        else:
            for s in range(ncut):
                arrive(p, s)
        adjoint_slice(p, total - 1, 3, 2, far_field(p))
        repeat(total - 1, backward)
        if per > 1:
            for k in range(gchunks):

                @pl.when(has_right)
                def _():
                    grad_copy(p, k).start()

    def far_field(p):
        out = sandwich(2, 3, exit_wave(p, total - 1))
        f_re, f_im = out[:, :width], out[:, width:]
        misfit = f_re * f_re + f_im * f_im - inten_v[p]
        return jnp.concatenate([(misfit * f_re).astype(BF16), (misfit * f_im).astype(BF16)], axis=0)

    for p in range(count):
        one_probe(p)

    @pl.when(has_right)
    def _():
        pos_copy.wait_send()
        for p in range(count):
            for k in range(gchunks):
                grad_copy(p, k).wait_send()

    for p in range(count):
        for k in range(chunks):
            for o in range(1, ncut):
                cross_copy(o, cut, p, k).wait_send()

    @pl.when(has_left)
    def _():
        for p in range(count):
            for k in range(chunks):
                strip_copy(p, k).wait_send()
        for p in range(count):
            for k in range(gchunks):
                grad_copy(p, k).wait_recv()


def place_kernel(own, strip, pos, left, out_hbm, out_v, sem):
    per, _, rows, cols = out_v.shape
    count, width = own.shape[0], own.shape[3]
    iota = lax.broadcasted_iota(jnp.int32, (LANE_ROWS, cols), 0)
    rest = width - LANE_ROWS

    def add(source, row, p, j, part):
        base = row // LANE_ROWS * LANE_ROWS
        shift = row - base
        body = pl.multiple_of(base + LANE_ROWS, LANE_ROWS)
        base = pl.multiple_of(base, LANE_ROWS)
        after = pl.multiple_of(jnp.minimum(base + width, rows - LANE_ROWS), LANE_ROWS)
        whole = source[p, j, part].astype(F32)
        out_v[j, part, pl.ds(body, rest), :] += whole[LANE_ROWS:]
        head = whole[:LANE_ROWS]
        out_v[j, part, pl.ds(base, LANE_ROWS), :] += jnp.where(iota >= shift, head, 0.0)
        out_v[j, part, pl.ds(after, LANE_ROWS), :] += jnp.where(iota < shift, head, 0.0)

    copies = []
    for j in range(per):
        for part in range(2):
            out_v[j, part] = jnp.zeros((rows, cols), F32)
            for p in range(count):
                add(own, pos[p, 0], p, j, part)
                add(strip, left[p, 0], p, j, part)
            copy = pltpu.make_async_copy(out_v.at[j, part], out_hbm.at[j, part], sem.at[j, part])
            copy.start()
            copies.append(copy)
    for copy in copies:
        copy.wait()


def per_device(tables, object_delta, probe_wave, intensity, positions):
    per, _, rows, cols = object_delta.shape
    count, width = intensity.shape[0], intensity.shape[1]
    ncut = lax.axis_size("cuts")
    chunks, gchunks, loads = 4, 2, 4
    anywhere = pl.BlockSpec(memory_space=pl.ANY)
    vmem = pl.BlockSpec(memory_space=pltpu.VMEM)
    smem = pl.BlockSpec(memory_space=pltpu.SMEM)
    dma = pltpu.SemaphoreType.DMA
    piece = (count, per, 2, width, cols)
    others = max(ncut - 1, 1)
    own, strip, left = pl.pallas_call(
        functools.partial(exchange_kernel, chunks=chunks, gchunks=gchunks),
        out_shape=(
            pltpu.VMEM(piece, F32),
            pltpu.VMEM(piece, BF16),
            jax.ShapeDtypeStruct(positions.shape, positions.dtype),
        ),
        in_specs=[anywhere, anywhere, anywhere, smem, anywhere],
        out_specs=(vmem, vmem, smem),
        scratch_shapes=[
            pltpu.VMEM((per, 2, rows // LANE_ROWS + 1, LANE_ROWS, cols), F32),
            pltpu.VMEM(probe_wave.shape, BF16),
            pltpu.VMEM(intensity.shape, F32),
            pltpu.VMEM(tables.shape, BF16),
            pltpu.VMEM(piece, BF16),
            pltpu.VMEM(piece, BF16),
            pltpu.VMEM((count, ncut, per, 2, width, cols), BF16),
            pltpu.VMEM((count, ncut * per, 2, width, cols), BF16),
            pltpu.VMEM((2 * width, cols), BF16),
            pltpu.VMEM(piece, BF16),
            dma((per, 2, loads)),
            dma((4,)),
            dma((2,)),
            dma((count, chunks)),
            dma((count, chunks)),
            dma((others, count, chunks)),
            dma((others, count, chunks)),
            dma((count, gchunks)),
            dma((count, gchunks)),
        ],
        compiler_params=pltpu.CompilerParams(collective_id=0, has_side_effects=True),
        name="exchange",
    )(
        object_delta.reshape(per, 2, rows // LANE_ROWS, LANE_ROWS, cols),
        probe_wave, intensity, positions, tables,
    )
    own = pltpu.with_memory_space_constraint(own, pltpu.VMEM)
    strip = pltpu.with_memory_space_constraint(strip, pltpu.VMEM)
    return pl.pallas_call(
        place_kernel,
        out_shape=jax.ShapeDtypeStruct(object_delta.shape, F32),
        in_specs=[vmem, vmem, smem, smem],
        out_specs=anywhere,
        scratch_shapes=[pltpu.VMEM(object_delta.shape, F32), dma((per, 2))],
        name="place",
    )(own, strip, positions, left)


def solution(mesh):
    def whole(object_delta, probe_wave, intensity, positions):
        tables = jnp.asarray(make_tables(probe_wave.shape[-1]))
        return jax.shard_map(
            per_device,
            mesh=mesh,
            in_specs=(
                P(),
                P("cuts", None, None, "tile"),
                P(),
                P("tile", None, None),
                P("tile", None),
            ),
            out_specs=P("cuts", None, None, "tile"),
            check_vma=False,
        )(tables, object_delta, probe_wave, intensity, positions)

    return whole
```

```python
import functools
import math

import jax
import jax.numpy as jnp
import numpy as np
from jax import lax
from jax.experimental import pallas as pl
from jax.experimental.pallas import tpu as pltpu
from jax.sharding import PartitionSpec as P

F32 = jnp.float32
BF16 = jnp.bfloat16
MESH = pl.DeviceIdType.MESH
LANE_ROWS = 8


def make_tables(width):
    counter = np.arange(width)
    phase = (counter[:, None] * counter[None, :] % width) * (2.0 * math.pi / width)
    four = np.exp(-1j * phase) / math.sqrt(width)
    signed = np.where(counter < width // 2, counter, counter - width).astype(np.float64)
    kernel = np.exp(-2j * math.pi / width * signed * signed)
    prop = np.conj(four) @ (kernel[:, None] * four)
    prop = 0.5 * (prop + prop.T)

    def block(table):
        re, im = table.real, table.imag
        return np.block([[re, -im], [im, re]])

    big = [block(prop), block(prop).T, block(four), block(four).T]
    return np.stack(big).astype(np.float32).astype(jnp.bfloat16)


def dot(a, b):
    return jnp.dot(a, b, preferred_element_type=F32)


def repeat(count, body):
    if count == 1:
        body(0)
    elif count > 1:
        lax.fori_loop(0, count, lambda i, _: (body(i), 0)[1], 0)


def exchange_kernel(
    obj_hbm, probe_hbm, inten_hbm, pos_hbm, tabs_hbm,
    own_out, got_out, meta_out, acc_out,
    pos, left_out, obj_v, probe_v, inten_v, tabs_v, edge_send, edge_recv, inten_send, inten_b,
    win, psi, wave, lam, grad_send,
    obj_sem, load_sem, pos_sem, e_ssem, e_rsem, x_ssem, x_rsem, g_ssem, g_rsem, i_ssem, i_rsem, go_sem,
    *, chunks, gchunks, early, ahead,
):
    cut, tile = lax.axis_index("cuts"), lax.axis_index("tile")
    ncut, ntile = lax.axis_size("cuts"), lax.axis_size("tile")
    per, cols = obj_v.shape[0], obj_v.shape[-1]
    groups = obj_hbm.shape[2]
    count, width = inten_v.shape[0], inten_v.shape[1]
    slots = 2 * count
    total = ncut * per
    height = width // chunks
    half = width // gchunks
    has_left, has_right = tile > 0, tile < ntile - 1
    last = jnp.logical_not(has_right)
    odd = lax.rem(tile, 2) == 1
    even = jnp.logical_not(odd)
    left, right = {"tile": tile - 1}, {"tile": tile + 1}
    loads = obj_sem.shape[-1]
    load_groups = groups // loads

    def obj_copy(j, part, q):
        span = pl.ds(q * load_groups, load_groups)
        return pltpu.make_async_copy(
            obj_hbm.at[j, part, span], obj_v.at[j, part, span], obj_sem.at[j, part, q]
        )

    probe_copy = pltpu.make_async_copy(probe_hbm, probe_v, load_sem.at[1])
    tabs_copy = pltpu.make_async_copy(tabs_hbm, tabs_v, load_sem.at[2])
    inten_copy = pltpu.make_async_copy(inten_hbm, inten_v, load_sem.at[3])
    here_copy = pltpu.make_async_copy(pos_hbm, pos, load_sem.at[0])
    here_copy.start()
    for j in range(per):
        for part in range(2):
            for q in range(loads):
                obj_copy(j, part, q).start()

    barrier = pltpu.get_barrier_semaphore()

    @pl.when(has_left)
    def _():
        pl.semaphore_signal(barrier, inc=1, device_id=left, device_id_type=MESH)

    @pl.when(has_right)
    def _():
        pl.semaphore_signal(barrier, inc=1, device_id=right, device_id_type=MESH)

    for o in range(1, ncut):
        peer = {"cuts": lax.rem(cut + o, ncut)}
        pl.semaphore_signal(barrier, inc=1, device_id=peer, device_id_type=MESH)
    peers = ncut - 1 + jnp.where(has_left, 1, 0) + jnp.where(has_right, 1, 0)
    here_copy.wait()
    pl.semaphore_wait(barrier, peers)

    pos_copy = pltpu.make_async_remote_copy(
        src_ref=pos, dst_ref=left_out, send_sem=pos_sem.at[0], recv_sem=pos_sem.at[1],
        device_id=right, device_id_type=MESH,
    )

    @pl.when(has_right)
    def _():
        pos_copy.start()

    lanes = lax.broadcasted_iota(jnp.int32, (height, cols), 1)
    glanes = lax.broadcasted_iota(jnp.int32, (half, cols), 1)
    first_lines = lax.broadcasted_iota(jnp.int32, (LANE_ROWS, cols), 0)

    def corner(slot):
        if slot < count:
            return left_out[slot, 0], left_out[slot, 1] - (tile - 1) * cols
        return pos[slot - count, 0], pos[slot - count, 1] - tile * cols

    def window_rows(row, j, part, k):
        base = lax.div(row, LANE_ROWS)
        part_groups = height // LANE_ROWS
        main = obj_v[j, part, pl.ds(base + k * part_groups, part_groups)].reshape(height, cols)
        if k > 0:
            return main
        wrapped = obj_v[j, part, base + width // LANE_ROWS]
        head = jnp.where(first_lines < row - base * LANE_ROWS, wrapped, main[:LANE_ROWS])
        return jnp.concatenate([head, main[LANE_ROWS:]], axis=0)

    def edge_copy(p, k):
        span = pl.ds(k * height, height)
        return pltpu.make_async_remote_copy(
            src_ref=edge_send.at[p, :, :, span, :], dst_ref=edge_recv.at[p, :, :, span, :],
            send_sem=e_ssem.at[p, k], recv_sem=e_rsem.at[p, k],
            device_id=right, device_id_type=MESH,
        )

    def inten_move(p):
        return pltpu.make_async_remote_copy(
            src_ref=inten_send.at[p], dst_ref=inten_b.at[p],
            send_sem=i_ssem.at[p], recv_sem=i_rsem.at[p],
            device_id=right, device_id_type=MESH,
        )

    def cross_copy(o, source, slot, k):
        span = pl.ds(k * height, height)
        part = win.at[slot, source, :, :, span, :]
        return pltpu.make_async_remote_copy(
            src_ref=part, dst_ref=part,
            send_sem=x_ssem.at[o - 1, slot, k], recv_sem=x_rsem.at[o - 1, slot, k],
            device_id={"cuts": lax.rem(cut + o, ncut)}, device_id_type=MESH,
        )

    def cross_start(slot, k):
        for o in range(1, ncut):
            cross_copy(o, cut, slot, k).start()

    def grad_copy(p, k):
        span = pl.ds(k * half, half)
        return pltpu.make_async_remote_copy(
            src_ref=grad_send.at[p, :, :, span, :], dst_ref=got_out.at[p, :, :, span, :],
            send_sem=g_ssem.at[p, k], recv_sem=g_rsem.at[p, k],
            device_id=left, device_id_type=MESH,
        )

    def merge(slot, k):
        row, col = corner(slot)
        span = pl.ds(k * height, height)
        for j in range(per):
            for part in range(2):
                cells = window_rows(row, j, part, k)
                if slot < count:
                    cells = jnp.where(
                        lanes < col, cells, edge_recv[slot, j, part, span, :].astype(F32)
                    )
                win[slot, cut, j, part, span, :] = cells.astype(BF16)

    for j in range(per):
        for part in range(2):
            for q in range(loads):
                obj_copy(j, part, q).wait()
            obj_v[j, part, groups] = jnp.zeros((LANE_ROWS, cols), F32)
    inten_copy.start()
    probe_copy.start()

    @pl.when(has_right)
    def _():
        for p in range(count):
            for k in range(chunks):
                for j in range(per):
                    for part in range(2):
                        edge_send[p, j, part, k * height : (k + 1) * height] = window_rows(
                            pos[p, 0], j, part, k
                        ).astype(BF16)
                edge_copy(p, k).start()

    @pl.when(last)
    def _():
        for slot in range(count, slots):
            for k in range(chunks):
                merge(slot, k)
                if slot == count:
                    cross_start(slot, k)

    inten_copy.wait()
    inten_send[...] = inten_v[...].astype(BF16)

    @pl.when(has_right)
    def _():
        for p in range(count):
            inten_move(p).start()

    @pl.when(last)
    def _():
        inten_b[count:slots] = inten_send[...]

    tabs_copy.start()

    @pl.when(jnp.logical_not(has_left))
    def _():
        for p in range(count):
            for d in range(2):
                left_out[p, d] = 0
        own_out[0:count] = jnp.zeros((count, *own_out.shape[1:]), F32)

    @pl.when(has_left)
    def _():
        pos_copy.wait_recv()
        for slot in range(count):
            for k in range(chunks):
                edge_copy(slot, k).wait_recv()
                merge(slot, k)
                if slot * chunks + k < early:
                    cross_start(slot, k)
                else:
                    pl.when(even)(lambda slot=slot, k=k: cross_start(slot, k))

    @pl.when(jnp.logical_and(even, has_left))
    def _():
        for i in range(ahead):
            for o in range(1, ncut):
                cross_copy(o, cut, i // chunks, i % chunks).wait_send()

    @pl.when(jnp.logical_and(even, has_right))
    def _():
        pl.semaphore_signal(go_sem, inc=1, device_id=right, device_id_type=MESH)

    probe_copy.wait()
    across = lax.broadcasted_iota(jnp.int32, (width, width), 1)
    down = lax.broadcasted_iota(jnp.int32, (width, width), 0)

    def illuminate(slot):
        row, col = corner(slot)
        shift = row - lax.div(row, LANE_ROWS) * LANE_ROWS
        source = across + shift
        move_rows = jnp.where(jnp.where(source >= width, source - width, source) == down, 1.0, 0.0)
        source = down + col
        move_cols = jnp.where(jnp.where(source >= width, source - width, source) == across, 1.0, 0.0)
        for part in range(2):
            rolled = dot(move_rows.astype(BF16), probe_v[part]).astype(BF16)
            psi[slot, 0, part] = dot(rolled, move_cols.astype(BF16)).astype(BF16)

    for slot in range(count):
        illuminate(slot)

    acc_out[...] = jnp.zeros_like(acc_out)
    for p in range(count):
        meta_out[2 * p] = jnp.full(meta_out.shape[1:], pos[p, 0], jnp.int32)
        meta_out[2 * p + 1] = jnp.full(meta_out.shape[1:], left_out[p, 0], jnp.int32)

    @pl.when(last)
    def _():
        for slot in range(count, slots):
            illuminate(slot)

    tabs_copy.wait()

    @pl.when(odd)
    def _():
        pl.semaphore_wait(go_sem, 1)
        for i in range(early, count * chunks):
            cross_start(i // chunks, i % chunks)

    @pl.when(last)
    def _():
        for slot in range(count + 1, slots):
            for k in range(chunks):
                cross_start(slot, k)

    def arrive(slot, owner):
        @pl.when(owner != cut)
        def _():
            o = lax.rem(cut - owner + ncut, ncut)
            for k in range(chunks):
                cross_copy(o, owner, slot, k).wait_recv()

    def stage(first, second, stacked, point):
        sides = []
        for b in range(gchunks):
            up, down = b * half, width + b * half
            rows_of = jnp.concatenate(
                [tabs_v[first, up : up + half], tabs_v[first, down : down + half]], axis=0
            )
            inner = dot(rows_of, stacked).astype(BF16)
            sides.append(jnp.concatenate([inner[:half], inner[half:]], axis=1))
        for b in range(gchunks):
            out = dot(sides[b], tabs_v[second])
            point(b, out[:, :width], out[:, width:])

    def put(ref, b, re, im):
        ref[pl.ds(b * half, half)] = re.astype(BF16)
        ref[pl.ds(width + b * half, half)] = im.astype(BF16)

    def transmission(slot, s, span):
        owner, j = s // per, lax.rem(s, per)
        return (
            1.0 + win[slot, owner, j, 0, span].astype(F32),
            win[slot, owner, j, 1, span].astype(F32),
        )

    def incident(slot, s, span):
        return psi[slot, s, 0, span].astype(F32), psi[slot, s, 1, span].astype(F32)

    def leave(slot, s):
        for b in range(gchunks):
            span = pl.ds(b * half, half)
            t_re, t_im = transmission(slot, s, span)
            p_re, p_im = incident(slot, s, span)
            put(wave, b, p_re * t_re - p_im * t_im, p_re * t_im + p_im * t_re)

    def adjoint_slice(slot, s, first, second, source):
        owner, j = s // per, lax.rem(s, per)
        foreign = slot < count
        p = jnp.where(foreign, slot, slot - count)
        col = jnp.where(
            foreign, left_out[p, 1] - (tile - 1) * cols, pos[p, 1] - tile * cols
        )
        low, high = jnp.where(foreign, 0, col), jnp.where(foreign, col, cols)

        @pl.when(owner == cut)
        def _():
            def gradient(b, m_re, m_im):
                span = pl.ds(b * half, half)
                p_re, p_im = incident(slot, s, span)
                g = (p_re * m_re + p_im * m_im, p_re * m_im - p_im * m_re)
                mine = jnp.logical_and(glanes >= low, glanes < high)
                for part in range(2):
                    own_out[slot, j, part, span, :] = jnp.where(mine, g[part], 0.0)
                    grad_send[slot, j, part, span, :] = jnp.where(mine, 0.0, g[part]).astype(BF16)
                if per == 1:

                    @pl.when(foreign)
                    def _():
                        grad_copy(slot, b).start()

            stage(first, second, source[...], gradient)

        @pl.when(s > cut * per)
        def _():
            def back(b, m_re, m_im):
                t_re, t_im = transmission(slot, s, pl.ds(b * half, half))
                put(wave, b, t_re * m_re + t_im * m_im, t_re * m_im - t_im * m_re)

            stage(first, second, source[...], back)

    def one_probe(slot):
        def forward(s):
            arrive(slot, s // per)
            leave(slot, s)

            def keep_wave(b, re, im):
                psi[slot, s + 1, 0, pl.ds(b * half, half)] = re.astype(BF16)
                psi[slot, s + 1, 1, pl.ds(b * half, half)] = im.astype(BF16)

            stage(0, 1, wave[...], keep_wave)

        def backward(i):
            s = total - 2 - i

            @pl.when(s >= cut * per)
            def _():
                adjoint_slice(slot, s, 1, 0, wave)

        if per == 1:
            repeat(total - 1, forward)
            arrive(slot, total - 1)
        else:
            for s in range(ncut):
                arrive(slot, s)
            for s in range(total - 1):
                leave(slot, s)

                def keep_wave(b, re, im, s=s):
                    psi[slot, s + 1, 0, pl.ds(b * half, half)] = re.astype(BF16)
                    psi[slot, s + 1, 1, pl.ds(b * half, half)] = im.astype(BF16)

                stage(0, 1, wave[...], keep_wave)
        leave(slot, total - 1)

        for p in range(count):
            pl.when(slot == p)(lambda p=p: inten_move(p).wait_recv())

        def misfit(b, re, im):
            gap = re * re + im * im - inten_b[slot, pl.ds(b * half, half)].astype(F32)
            put(lam, b, gap * re, gap * im)

        stage(2, 3, wave[...], misfit)
        adjoint_slice(slot, total - 1, 3, 2, lam)
        repeat(total - 1, backward)
        if per > 1:
            for b in range(gchunks):

                @pl.when(slot < count)
                def _():
                    grad_copy(slot, b).start()

    def turn(i, _):
        final = jnp.where(i == 0, count, jnp.where(i <= count, i - 1, i))
        one_probe(jnp.where(has_right, i, final))
        return 0

    turns = jnp.where(has_left, count, 0) + jnp.where(has_right, 0, count)
    lax.fori_loop(0, turns, turn, 0)

    @pl.when(last)
    def _():
        for slot in range(count, slots):
            got_out[slot - count] = own_out[slot].astype(BF16)

    def cross_drain(slot):
        for k in range(chunks):
            for o in range(1, ncut):
                cross_copy(o, cut, slot, k).wait_send()

    @pl.when(last)
    def _():
        for slot in range(count, slots):
            cross_drain(slot)

    @pl.when(has_right)
    def _():
        pos_copy.wait_send()
        for p in range(count):
            inten_move(p).wait_send()
            for k in range(chunks):
                edge_copy(p, k).wait_send()
        for p in range(count):
            for k in range(gchunks):
                grad_copy(p, k).wait_recv()

    @pl.when(has_left)
    def _():
        for slot in range(count):
            for k in range(chunks):

                @pl.when(jnp.logical_or(odd, slot * chunks + k >= ahead))
                def _():
                    for o in range(1, ncut):
                        cross_copy(o, cut, slot, k).wait_send()

            for k in range(gchunks):
                grad_copy(slot, k).wait_send()


def place_kernel(own, got, meta, _, out_hbm, out_v, sem):
    per, _, rows, cols = out_v.shape
    count, width = got.shape[0], got.shape[3]
    iota = lax.broadcasted_iota(jnp.int32, (LANE_ROWS, cols), 0)

    step = width // 4

    def add(source, row, p, j, part):
        base = row // LANE_ROWS * LANE_ROWS
        shift = row - base
        after = pl.multiple_of(jnp.minimum(base + width, rows - LANE_ROWS), LANE_ROWS)
        head = source[p, j, part, :16].astype(F32)[:LANE_ROWS]
        for r in range(4):
            cells = source[p, j, part, r * step : (r + 1) * step].astype(F32)
            if r == 0:
                cells = jnp.concatenate(
                    [jnp.where(iota >= shift, cells[:LANE_ROWS], 0.0), cells[LANE_ROWS:]], axis=0
                )
            at = pl.ds(pl.multiple_of(base + r * step, LANE_ROWS), step)
            out_v[j, part, at, :] += cells
        out_v[j, part, pl.ds(after, LANE_ROWS), :] += jnp.where(iota < shift, head, 0.0)

    blocks = sem.shape[-1]
    span = rows // blocks
    corners = [jnp.max(meta[i]) for i in range(2 * count)]

    def touched(b):
        hit = False
        for row in corners:
            near = jnp.logical_and(row < (b + 1) * span, row + width + LANE_ROWS > b * span)
            hit = jnp.logical_or(hit, near)
        return hit

    def block_copy(j, part, b):
        at = pl.ds(b * span, span)
        return pltpu.make_async_copy(
            out_v.at[j, part, at, :], out_hbm.at[j, part, at, :], sem.at[j, part, b]
        )

    busy = [touched(b) for b in range(blocks)]
    for j in range(per):
        for part in range(2):
            for b in range(blocks):
                pl.when(jnp.logical_not(busy[b]))(lambda: block_copy(j, part, b).start())
    for j in range(per):
        for part in range(2):
            for p in range(count):
                add(own, corners[2 * p + 1], p, j, part)
                add(got, corners[2 * p], p, j, part)
            for b in range(blocks):
                pl.when(busy[b])(lambda: block_copy(j, part, b).start())
    for j in range(per):
        for part in range(2):
            for b in range(blocks):
                block_copy(j, part, b).wait()


def per_device(tables, object_delta, probe_wave, intensity, positions):
    per, _, rows, cols = object_delta.shape
    count, width = intensity.shape[0], intensity.shape[1]
    ncut = lax.axis_size("cuts")
    chunks, gchunks, loads, early, ahead = 4, 2, 4, 2, 6
    anywhere = pl.BlockSpec(memory_space=pl.ANY)
    vmem = pl.BlockSpec(memory_space=pltpu.VMEM)
    dma = pltpu.SemaphoreType.DMA
    piece = (count, per, 2, width, cols)
    others = max(ncut - 1, 1)
    slots = 2 * count
    own, got, meta, acc = pl.pallas_call(
        functools.partial(exchange_kernel, chunks=chunks, gchunks=gchunks, early=early, ahead=ahead),
        out_shape=(
            pltpu.VMEM((slots, *piece[1:]), F32),
            pltpu.VMEM(piece, BF16),
            pltpu.VMEM((2 * count, LANE_ROWS, 128), jnp.int32),
            pltpu.VMEM(object_delta.shape, F32),
        ),
        in_specs=[anywhere] * 5,
        out_specs=(vmem, vmem, vmem, vmem),
        scratch_shapes=[
            pltpu.SMEM(positions.shape, positions.dtype),
            pltpu.SMEM(positions.shape, positions.dtype),
            pltpu.VMEM((per, 2, rows // LANE_ROWS + 1, LANE_ROWS, cols), F32),
            pltpu.VMEM(probe_wave.shape, BF16),
            pltpu.VMEM(intensity.shape, F32),
            pltpu.VMEM(tables.shape, BF16),
            pltpu.VMEM(piece, BF16),
            pltpu.VMEM(piece, BF16),
            pltpu.VMEM(intensity.shape, BF16),
            pltpu.VMEM((slots, width, cols), BF16),
            pltpu.VMEM((slots, ncut, per, 2, width, cols), BF16),
            pltpu.VMEM((slots, ncut * per, 2, width, cols), BF16),
            pltpu.VMEM((2 * width, cols), BF16),
            pltpu.VMEM((2 * width, cols), BF16),
            pltpu.VMEM((slots, *piece[1:]), BF16),
            dma((per, 2, loads)),
            dma((4,)),
            dma((2,)),
            dma((count, chunks)),
            dma((count, chunks)),
            dma((others, slots, chunks)),
            dma((others, slots, chunks)),
            dma((count, gchunks)),
            dma((count, gchunks)),
            dma((count,)),
            dma((count,)),
            pltpu.SemaphoreType.REGULAR,
        ],
        compiler_params=pltpu.CompilerParams(
            collective_id=0, has_side_effects=True, vmem_limit_bytes=56 << 20
        ),
        name="exchange",
    )(
        object_delta.reshape(per, 2, rows // LANE_ROWS, LANE_ROWS, cols),
        probe_wave, intensity, positions, tables,
    )
    own = pltpu.with_memory_space_constraint(own, pltpu.VMEM)
    got = pltpu.with_memory_space_constraint(got, pltpu.VMEM)
    acc = pltpu.with_memory_space_constraint(acc, pltpu.VMEM)
    meta = pltpu.with_memory_space_constraint(meta, pltpu.VMEM)
    placed, _ = pl.pallas_call(
        place_kernel,
        out_shape=(
            jax.ShapeDtypeStruct(object_delta.shape, F32),
            pltpu.VMEM(object_delta.shape, F32),
        ),
        in_specs=[vmem, vmem, vmem, vmem],
        out_specs=(anywhere, vmem),
        scratch_shapes=[dma((per, 2, 4))],
        compiler_params=pltpu.CompilerParams(vmem_limit_bytes=56 << 20),
        input_output_aliases={3: 1},
        name="place",
    )(own, got, meta, acc)
    return placed


def solution(mesh):
    def whole(object_delta, probe_wave, intensity, positions):
        tables = jnp.asarray(make_tables(probe_wave.shape[-1]))
        return jax.shard_map(
            per_device,
            mesh=mesh,
            in_specs=(
                P(),
                P("cuts", None, None, "tile"),
                P(),
                P("tile", None, None),
                P("tile", None),
            ),
            out_specs=P("cuts", None, None, "tile"),
            check_vma=False,
        )(tables, object_delta, probe_wave, intensity, positions)

    return whole
```

```python
import functools
import math

import jax
import jax.numpy as jnp
import numpy as np
from jax import lax
from jax.experimental import pallas as pl
from jax.experimental.pallas import tpu as pltpu
from jax.sharding import PartitionSpec as P

F32 = jnp.float32
BF16 = jnp.bfloat16
MESH = pl.DeviceIdType.MESH
LANE_ROWS = 8


def make_tables(width):
    counter = np.arange(width)
    phase = (counter[:, None] * counter[None, :] % width) * (2.0 * math.pi / width)
    four = np.exp(-1j * phase) / math.sqrt(width)
    signed = np.where(counter < width // 2, counter, counter - width).astype(np.float64)
    kernel = np.exp(-2j * math.pi / width * signed * signed)
    prop = np.conj(four) @ (kernel[:, None] * four)
    prop = 0.5 * (prop + prop.T)

    def block(table):
        re, im = table.real, table.imag
        return np.block([[re, -im], [im, re]])

    big = [block(prop), block(prop).T, block(four), block(four).T]
    return np.stack(big).astype(np.float32).astype(jnp.bfloat16)


def dot(a, b):
    return jnp.dot(a, b, preferred_element_type=F32)


def repeat(count, body):
    if count == 1:
        body(0)
    elif count > 1:
        lax.fori_loop(0, count, lambda i, _: (body(i), 0)[1], 0)


def exchange_kernel(
    obj_hbm, probe_hbm, inten_hbm, pos_hbm, tabs_hbm,
    own_out, got_out, meta_out, acc_out,
    pos, left_out, obj_v, probe_v, inten_v, tabs_v, edge_send, edge_recv, inten_send, inten_b,
    win, psi, wave, lam, grad_send,
    obj_sem, load_sem, pos_sem, e_ssem, e_rsem, x_ssem, x_rsem, g_ssem, g_rsem, i_ssem, i_rsem, go_sem,
    *, chunks, gchunks, early,
):
    cut, tile = lax.axis_index("cuts"), lax.axis_index("tile")
    ncut, ntile = lax.axis_size("cuts"), lax.axis_size("tile")
    per, cols = obj_v.shape[0], obj_v.shape[-1]
    groups = obj_hbm.shape[2]
    count, width = inten_v.shape[0], inten_v.shape[1]
    slots = 2 * count
    total = ncut * per
    height = width // chunks
    half = width // gchunks
    has_left, has_right = tile > 0, tile < ntile - 1
    last = jnp.logical_not(has_right)
    odd = lax.rem(tile, 2) == 1
    even = jnp.logical_not(odd)
    left, right = {"tile": tile - 1}, {"tile": tile + 1}
    loads = obj_sem.shape[-1]
    load_groups = groups // loads

    def obj_copy(j, part, q):
        span = pl.ds(q * load_groups, load_groups)
        return pltpu.make_async_copy(
            obj_hbm.at[j, part, span], obj_v.at[j, part, span], obj_sem.at[j, part, q]
        )

    probe_copy = pltpu.make_async_copy(probe_hbm, probe_v, load_sem.at[1])
    tabs_copy = pltpu.make_async_copy(tabs_hbm, tabs_v, load_sem.at[2])
    inten_copy = pltpu.make_async_copy(inten_hbm, inten_v, load_sem.at[3])
    here_copy = pltpu.make_async_copy(pos_hbm, pos, load_sem.at[0])
    here_copy.start()
    for j in range(per):
        for part in range(2):
            for q in range(loads):
                obj_copy(j, part, q).start()

    barrier = pltpu.get_barrier_semaphore()

    @pl.when(has_left)
    def _():
        pl.semaphore_signal(barrier, inc=1, device_id=left, device_id_type=MESH)

    @pl.when(has_right)
    def _():
        pl.semaphore_signal(barrier, inc=1, device_id=right, device_id_type=MESH)

    for o in range(1, ncut):
        peer = {"cuts": lax.rem(cut + o, ncut)}
        pl.semaphore_signal(barrier, inc=1, device_id=peer, device_id_type=MESH)
    peers = ncut - 1 + jnp.where(has_left, 1, 0) + jnp.where(has_right, 1, 0)
    here_copy.wait()
    pl.semaphore_wait(barrier, peers)

    pos_copy = pltpu.make_async_remote_copy(
        src_ref=pos, dst_ref=left_out, send_sem=pos_sem.at[0], recv_sem=pos_sem.at[1],
        device_id=right, device_id_type=MESH,
    )

    @pl.when(has_right)
    def _():
        pos_copy.start()

    lanes = lax.broadcasted_iota(jnp.int32, (height, cols), 1)
    glanes = lax.broadcasted_iota(jnp.int32, (half, cols), 1)
    first_lines = lax.broadcasted_iota(jnp.int32, (LANE_ROWS, cols), 0)

    def corner(slot):
        if slot < count:
            return left_out[slot, 0], left_out[slot, 1] - (tile - 1) * cols
        return pos[slot - count, 0], pos[slot - count, 1] - tile * cols

    def window_rows(row, j, part, k):
        base = lax.div(row, LANE_ROWS)
        part_groups = height // LANE_ROWS
        main = obj_v[j, part, pl.ds(base + k * part_groups, part_groups)].reshape(height, cols)
        if k > 0:
            return main
        wrapped = obj_v[j, part, base + width // LANE_ROWS]
        head = jnp.where(first_lines < row - base * LANE_ROWS, wrapped, main[:LANE_ROWS])
        return jnp.concatenate([head, main[LANE_ROWS:]], axis=0)

    def edge_copy(p, k):
        span = pl.ds(k * height, height)
        return pltpu.make_async_remote_copy(
            src_ref=edge_send.at[p, :, :, span, :], dst_ref=edge_recv.at[p, :, :, span, :],
            send_sem=e_ssem.at[p, k], recv_sem=e_rsem.at[p, k],
            device_id=right, device_id_type=MESH,
        )

    def inten_move(p):
        return pltpu.make_async_remote_copy(
            src_ref=inten_send.at[p], dst_ref=inten_b.at[p],
            send_sem=i_ssem.at[p], recv_sem=i_rsem.at[p],
            device_id=right, device_id_type=MESH,
        )

    def cross_copy(o, source, slot, k):
        span = pl.ds(k * height, height)
        part = win.at[slot, source, :, :, span, :]
        return pltpu.make_async_remote_copy(
            src_ref=part, dst_ref=part,
            send_sem=x_ssem.at[o - 1, slot, k], recv_sem=x_rsem.at[o - 1, slot, k],
            device_id={"cuts": lax.rem(cut + o, ncut)}, device_id_type=MESH,
        )

    def cross_start(slot, k):
        for o in range(1, ncut):
            cross_copy(o, cut, slot, k).start()

    def grad_copy(p, k):
        span = pl.ds(k * half, half)
        return pltpu.make_async_remote_copy(
            src_ref=grad_send.at[p, :, :, span, :], dst_ref=got_out.at[p, :, :, span, :],
            send_sem=g_ssem.at[p, k], recv_sem=g_rsem.at[p, k],
            device_id=left, device_id_type=MESH,
        )

    def merge(slot, k):
        row, col = corner(slot)
        span = pl.ds(k * height, height)
        for j in range(per):
            for part in range(2):
                cells = window_rows(row, j, part, k)
                if slot < count:
                    cells = jnp.where(
                        lanes < col, cells, edge_recv[slot, j, part, span, :].astype(F32)
                    )
                win[slot, cut, j, part, span, :] = cells.astype(BF16)

    for j in range(per):
        for part in range(2):
            for q in range(loads):
                obj_copy(j, part, q).wait()
            obj_v[j, part, groups] = jnp.zeros((LANE_ROWS, cols), F32)
    inten_copy.start()
    probe_copy.start()

    @pl.when(has_right)
    def _():
        for p in range(count):
            for k in range(chunks):
                for j in range(per):
                    for part in range(2):
                        edge_send[p, j, part, k * height : (k + 1) * height] = window_rows(
                            pos[p, 0], j, part, k
                        ).astype(BF16)
                edge_copy(p, k).start()

    @pl.when(last)
    def _():
        for slot in range(count, slots):
            for k in range(chunks):
                merge(slot, k)
                if slot == count:
                    cross_start(slot, k)

    inten_copy.wait()
    inten_send[...] = inten_v[...].astype(BF16)

    @pl.when(has_right)
    def _():
        for p in range(count):
            inten_move(p).start()

    @pl.when(last)
    def _():
        inten_b[count:slots] = inten_send[...]

    tabs_copy.start()

    @pl.when(jnp.logical_not(has_left))
    def _():
        for p in range(count):
            for d in range(2):
                left_out[p, d] = 0
        own_out[0:count] = jnp.zeros((count, *own_out.shape[1:]), F32)

    @pl.when(has_left)
    def _():
        pos_copy.wait_recv()

    across = lax.broadcasted_iota(jnp.int32, (width, width), 1)
    down = lax.broadcasted_iota(jnp.int32, (width, width), 0)

    def illuminate(slot):
        row, col = corner(slot)
        shift = row - lax.div(row, LANE_ROWS) * LANE_ROWS
        source = across + shift
        move_rows = jnp.where(jnp.where(source >= width, source - width, source) == down, 1.0, 0.0)
        source = down + col
        move_cols = jnp.where(jnp.where(source >= width, source - width, source) == across, 1.0, 0.0)
        for part in range(2):
            rolled = dot(move_rows.astype(BF16), probe_v[part]).astype(BF16)
            psi[slot, 0, part] = dot(rolled, move_cols.astype(BF16)).astype(BF16)

    def prepare():
        probe_copy.wait()
        for slot in range(count):
            illuminate(slot)

        acc_out[...] = jnp.zeros_like(acc_out)
        for p in range(count):
            meta_out[2 * p] = jnp.full(meta_out.shape[1:], pos[p, 0], jnp.int32)
            meta_out[2 * p + 1] = jnp.full(meta_out.shape[1:], left_out[p, 0], jnp.int32)

        @pl.when(last)
        def _():
            for slot in range(count, slots):
                illuminate(slot)

    pl.when(even)(prepare)

    @pl.when(has_left)
    def _():
        for slot in range(count):
            for k in range(chunks):
                edge_copy(slot, k).wait_recv()
                merge(slot, k)
                if slot * chunks + k < early:
                    cross_start(slot, k)
                else:
                    pl.when(even)(lambda slot=slot, k=k: cross_start(slot, k))

    def go():
        pl.semaphore_signal(go_sem, inc=1, device_id=right, device_id_type=MESH)

    leads = jnp.logical_and(even, has_right)
    pl.when(jnp.logical_and(leads, jnp.logical_not(has_left)))(go)

    pl.when(odd)(prepare)

    tabs_copy.wait()

    @pl.when(odd)
    def _():
        pl.semaphore_wait(go_sem, 1)
        for i in range(early, count * chunks):
            cross_start(i // chunks, i % chunks)

    @pl.when(last)
    def _():
        for slot in range(count + 1, slots):
            for k in range(chunks):
                cross_start(slot, k)

    def arrive(slot, owner):
        @pl.when(owner != cut)
        def _():
            o = lax.rem(cut - owner + ncut, ncut)
            for k in range(chunks):
                cross_copy(o, owner, slot, k).wait_recv()

    def stage(first, second, stacked, point):
        sides = []
        for b in range(gchunks):
            up, down = b * half, width + b * half
            rows_of = jnp.concatenate(
                [tabs_v[first, up : up + half], tabs_v[first, down : down + half]], axis=0
            )
            inner = dot(rows_of, stacked).astype(BF16)
            sides.append(jnp.concatenate([inner[:half], inner[half:]], axis=1))
        for b in range(gchunks):
            out = dot(sides[b], tabs_v[second])
            point(b, out[:, :width], out[:, width:])

    def put(ref, b, re, im):
        ref[pl.ds(b * half, half)] = re.astype(BF16)
        ref[pl.ds(width + b * half, half)] = im.astype(BF16)

    def transmission(slot, s, span):
        owner, j = s // per, lax.rem(s, per)
        return (
            1.0 + win[slot, owner, j, 0, span].astype(F32),
            win[slot, owner, j, 1, span].astype(F32),
        )

    def incident(slot, s, span):
        return psi[slot, s, 0, span].astype(F32), psi[slot, s, 1, span].astype(F32)

    def leave(slot, s):
        for b in range(gchunks):
            span = pl.ds(b * half, half)
            t_re, t_im = transmission(slot, s, span)
            p_re, p_im = incident(slot, s, span)
            put(wave, b, p_re * t_re - p_im * t_im, p_re * t_im + p_im * t_re)

    def adjoint_slice(slot, s, first, second, source):
        owner, j = s // per, lax.rem(s, per)
        foreign = slot < count
        p = jnp.where(foreign, slot, slot - count)
        col = jnp.where(
            foreign, left_out[p, 1] - (tile - 1) * cols, pos[p, 1] - tile * cols
        )
        low, high = jnp.where(foreign, 0, col), jnp.where(foreign, col, cols)

        @pl.when(owner == cut)
        def _():
            def gradient(b, m_re, m_im):
                span = pl.ds(b * half, half)
                p_re, p_im = incident(slot, s, span)
                g = (p_re * m_re + p_im * m_im, p_re * m_im - p_im * m_re)
                mine = jnp.logical_and(glanes >= low, glanes < high)
                for part in range(2):
                    own_out[slot, j, part, span, :] = jnp.where(mine, g[part], 0.0)
                    grad_send[slot, j, part, span, :] = jnp.where(mine, 0.0, g[part]).astype(BF16)
                if per == 1:

                    @pl.when(foreign)
                    def _():
                        grad_copy(slot, b).start()

                @pl.when(jnp.logical_not(foreign))
                def _():
                    for part in range(2):
                        got_out[p, j, part, span, :] = jnp.where(mine, g[part], 0.0).astype(BF16)

            stage(first, second, source[...], gradient)

        @pl.when(s > cut * per)
        def _():
            def back(b, m_re, m_im):
                t_re, t_im = transmission(slot, s, pl.ds(b * half, half))
                put(wave, b, t_re * m_re + t_im * m_im, t_re * m_im - t_im * m_re)

            stage(first, second, source[...], back)

    def one_probe(slot):
        def forward(s):
            arrive(slot, s // per)
            leave(slot, s)

            def keep_wave(b, re, im):
                psi[slot, s + 1, 0, pl.ds(b * half, half)] = re.astype(BF16)
                psi[slot, s + 1, 1, pl.ds(b * half, half)] = im.astype(BF16)

            stage(0, 1, wave[...], keep_wave)

        def backward(i):
            s = total - 2 - i

            @pl.when(s >= cut * per)
            def _():
                adjoint_slice(slot, s, 1, 0, wave)

        if per == 1:
            repeat(total - 1, forward)
            arrive(slot, total - 1)
        else:
            for s in range(ncut):
                arrive(slot, s)
            for s in range(total - 1):
                leave(slot, s)

                def keep_wave(b, re, im, s=s):
                    psi[slot, s + 1, 0, pl.ds(b * half, half)] = re.astype(BF16)
                    psi[slot, s + 1, 1, pl.ds(b * half, half)] = im.astype(BF16)

                stage(0, 1, wave[...], keep_wave)
        leave(slot, total - 1)

        for p in range(count):
            pl.when(slot == p)(lambda p=p: inten_move(p).wait_recv())

        def misfit(b, re, im):
            gap = re * re + im * im - inten_b[slot, pl.ds(b * half, half)].astype(F32)
            put(lam, b, gap * re, gap * im)

        pl.when(jnp.logical_and(leads, slot == 0))(go)
        stage(2, 3, wave[...], misfit)
        adjoint_slice(slot, total - 1, 3, 2, lam)
        repeat(total - 1, backward)
        if per > 1:
            for b in range(gchunks):

                @pl.when(slot < count)
                def _():
                    grad_copy(slot, b).start()

    def turn(i, _):
        final = jnp.where(i == 0, count, jnp.where(i <= count, i - 1, i))
        one_probe(jnp.where(has_right, i, final))
        return 0

    turns = jnp.where(has_left, count, 0) + jnp.where(has_right, 0, count)
    lax.fori_loop(0, turns, turn, 0)

    def cross_drain(slot):
        for k in range(chunks):
            for o in range(1, ncut):
                cross_copy(o, cut, slot, k).wait_send()

    @pl.when(last)
    def _():
        for slot in range(count, slots):
            cross_drain(slot)

    @pl.when(has_right)
    def _():
        pos_copy.wait_send()
        for p in range(count):
            inten_move(p).wait_send()
            for k in range(chunks):
                edge_copy(p, k).wait_send()
        for p in range(count):
            for k in range(gchunks):
                grad_copy(p, k).wait_recv()

    @pl.when(has_left)
    def _():
        for slot in range(count):
            for k in range(chunks):

                for o in range(1, ncut):
                    cross_copy(o, cut, slot, k).wait_send()

            for k in range(gchunks):
                grad_copy(slot, k).wait_send()


def place_kernel(own, got, meta, _, out_hbm, out_v, sem):
    per, _, rows, cols = out_v.shape
    count, width = got.shape[0], got.shape[3]
    iota = lax.broadcasted_iota(jnp.int32, (LANE_ROWS, cols), 0)

    step = width // 4

    def add(source, row, p, j, part):
        base = row // LANE_ROWS * LANE_ROWS
        shift = row - base
        after = pl.multiple_of(jnp.minimum(base + width, rows - LANE_ROWS), LANE_ROWS)
        head = source[p, j, part, :16].astype(F32)[:LANE_ROWS]
        for r in range(4):
            cells = source[p, j, part, r * step : (r + 1) * step].astype(F32)
            if r == 0:
                cells = jnp.concatenate(
                    [jnp.where(iota >= shift, cells[:LANE_ROWS], 0.0), cells[LANE_ROWS:]], axis=0
                )
            at = pl.ds(pl.multiple_of(base + r * step, LANE_ROWS), step)
            out_v[j, part, at, :] += cells
        out_v[j, part, pl.ds(after, LANE_ROWS), :] += jnp.where(iota < shift, head, 0.0)

    blocks = sem.shape[-1]
    span = rows // blocks
    corners = [jnp.max(meta[i]) for i in range(2 * count)]

    def touched(b):
        hit = False
        for row in corners:
            near = jnp.logical_and(row < (b + 1) * span, row + width + LANE_ROWS > b * span)
            hit = jnp.logical_or(hit, near)
        return hit

    def block_copy(j, part, b):
        at = pl.ds(b * span, span)
        return pltpu.make_async_copy(
            out_v.at[j, part, at, :], out_hbm.at[j, part, at, :], sem.at[j, part, b]
        )

    busy = [touched(b) for b in range(blocks)]
    for j in range(per):
        for part in range(2):
            for b in range(blocks):
                pl.when(jnp.logical_not(busy[b]))(lambda: block_copy(j, part, b).start())
    for j in range(per):
        for part in range(2):
            for p in range(count):
                add(own, corners[2 * p + 1], p, j, part)
                add(got, corners[2 * p], p, j, part)
            for b in range(blocks):
                pl.when(busy[b])(lambda: block_copy(j, part, b).start())
    for j in range(per):
        for part in range(2):
            for b in range(blocks):
                block_copy(j, part, b).wait()


def per_device(tables, object_delta, probe_wave, intensity, positions):
    per, _, rows, cols = object_delta.shape
    count, width = intensity.shape[0], intensity.shape[1]
    ncut = lax.axis_size("cuts")
    chunks, gchunks, loads, early = 4, 2, 4, 2
    anywhere = pl.BlockSpec(memory_space=pl.ANY)
    vmem = pl.BlockSpec(memory_space=pltpu.VMEM)
    dma = pltpu.SemaphoreType.DMA
    piece = (count, per, 2, width, cols)
    others = max(ncut - 1, 1)
    slots = 2 * count
    own, got, meta, acc = pl.pallas_call(
        functools.partial(exchange_kernel, chunks=chunks, gchunks=gchunks, early=early),
        out_shape=(
            pltpu.VMEM((slots, *piece[1:]), F32),
            pltpu.VMEM(piece, BF16),
            pltpu.VMEM((2 * count, LANE_ROWS, 128), jnp.int32),
            pltpu.VMEM(object_delta.shape, F32),
        ),
        in_specs=[anywhere] * 5,
        out_specs=(vmem, vmem, vmem, vmem),
        scratch_shapes=[
            pltpu.SMEM(positions.shape, positions.dtype),
            pltpu.SMEM(positions.shape, positions.dtype),
            pltpu.VMEM((per, 2, rows // LANE_ROWS + 1, LANE_ROWS, cols), F32),
            pltpu.VMEM(probe_wave.shape, BF16),
            pltpu.VMEM(intensity.shape, F32),
            pltpu.VMEM(tables.shape, BF16),
            pltpu.VMEM(piece, BF16),
            pltpu.VMEM(piece, BF16),
            pltpu.VMEM(intensity.shape, BF16),
            pltpu.VMEM((slots, width, cols), BF16),
            pltpu.VMEM((slots, ncut, per, 2, width, cols), BF16),
            pltpu.VMEM((slots, ncut * per, 2, width, cols), BF16),
            pltpu.VMEM((2 * width, cols), BF16),
            pltpu.VMEM((2 * width, cols), BF16),
            pltpu.VMEM((slots, *piece[1:]), BF16),
            dma((per, 2, loads)),
            dma((4,)),
            dma((2,)),
            dma((count, chunks)),
            dma((count, chunks)),
            dma((others, slots, chunks)),
            dma((others, slots, chunks)),
            dma((count, gchunks)),
            dma((count, gchunks)),
            dma((count,)),
            dma((count,)),
            pltpu.SemaphoreType.REGULAR,
        ],
        compiler_params=pltpu.CompilerParams(
            collective_id=0, has_side_effects=True, vmem_limit_bytes=56 << 20
        ),
        name="exchange",
    )(
        object_delta.reshape(per, 2, rows // LANE_ROWS, LANE_ROWS, cols),
        probe_wave, intensity, positions, tables,
    )
    own = pltpu.with_memory_space_constraint(own, pltpu.VMEM)
    got = pltpu.with_memory_space_constraint(got, pltpu.VMEM)
    acc = pltpu.with_memory_space_constraint(acc, pltpu.VMEM)
    meta = pltpu.with_memory_space_constraint(meta, pltpu.VMEM)
    placed, _ = pl.pallas_call(
        place_kernel,
        out_shape=(
            jax.ShapeDtypeStruct(object_delta.shape, F32),
            pltpu.VMEM(object_delta.shape, F32),
        ),
        in_specs=[vmem, vmem, vmem, vmem],
        out_specs=(anywhere, vmem),
        scratch_shapes=[dma((per, 2, 4))],
        compiler_params=pltpu.CompilerParams(vmem_limit_bytes=56 << 20),
        input_output_aliases={3: 1},
        name="place",
    )(own, got, meta, acc)
    return placed


def solution(mesh):
    def whole(object_delta, probe_wave, intensity, positions):
        tables = jnp.asarray(make_tables(probe_wave.shape[-1]))
        return jax.shard_map(
            per_device,
            mesh=mesh,
            in_specs=(
                P(),
                P("cuts", None, None, "tile"),
                P(),
                P("tile", None, None),
                P("tile", None),
            ),
            out_specs=P("cuts", None, None, "tile"),
            check_vma=False,
        )(tables, object_delta, probe_wave, intensity, positions)

    return whole
```

```python
import functools
import math

import jax
import jax.numpy as jnp
import numpy as np
from jax import lax
from jax.experimental import pallas as pl
from jax.experimental.pallas import tpu as pltpu
from jax.sharding import PartitionSpec as P

F32 = jnp.float32
BF16 = jnp.bfloat16
MESH = pl.DeviceIdType.MESH
LANE_ROWS = 8


def make_tables(width):
    counter = np.arange(width)
    phase = (counter[:, None] * counter[None, :] % width) * (2.0 * math.pi / width)
    four = np.exp(-1j * phase) / math.sqrt(width)
    signed = np.where(counter < width // 2, counter, counter - width).astype(np.float64)
    kernel = np.exp(-2j * math.pi / width * signed * signed)
    prop = np.conj(four) @ (kernel[:, None] * four)
    prop = 0.5 * (prop + prop.T)

    def block(table):
        re, im = table.real, table.imag
        return np.block([[re, -im], [im, re]])

    big = [block(prop), block(prop).T, block(four), block(four).T]
    return np.stack(big).astype(np.float32).astype(jnp.bfloat16)


def dot(a, b):
    return jnp.dot(a, b, preferred_element_type=F32)


def repeat(count, body):
    if count == 1:
        body(0)
    elif count > 1:
        lax.fori_loop(0, count, lambda i, _: (body(i), 0)[1], 0)


def exchange_kernel(
    obj_hbm, probe_hbm, inten_hbm, pos_hbm, tabs_hbm,
    own_out, got_out, meta_out, acc_out,
    pos, left_out, obj_v, probe_v, inten_v, tabs_v, edge_send, edge_recv, inten_send, inten_b,
    win, psi, wave, lam, grad_send, back_send,
    obj_sem, load_sem, pos_sem, e_ssem, e_rsem, x_ssem, x_rsem, g_ssem, g_rsem, i_ssem, i_rsem, r_ssem, r_rsem, go_sem,
    *, chunks, gchunks, early,
):
    cut, tile = lax.axis_index("cuts"), lax.axis_index("tile")
    ncut, ntile = lax.axis_size("cuts"), lax.axis_size("tile")
    per, cols = obj_v.shape[0], obj_v.shape[-1]
    groups = obj_hbm.shape[2]
    count, width = inten_v.shape[0], inten_v.shape[1]
    slots = 2 * count
    total = ncut * per
    height = width // chunks
    half = width // gchunks
    has_left, has_right = tile > 0, tile < ntile - 1
    last = jnp.logical_not(has_right)
    odd = lax.rem(tile, 2) == 1
    even = jnp.logical_not(odd)
    left, right = {"tile": tile - 1}, {"tile": tile + 1}
    loads = obj_sem.shape[-1]
    load_groups = groups // loads

    def obj_copy(j, part, q):
        span = pl.ds(q * load_groups, load_groups)
        return pltpu.make_async_copy(
            obj_hbm.at[j, part, span], obj_v.at[j, part, span], obj_sem.at[j, part, q]
        )

    probe_copy = pltpu.make_async_copy(probe_hbm, probe_v, load_sem.at[1])
    tabs_copy = pltpu.make_async_copy(tabs_hbm, tabs_v, load_sem.at[2])
    inten_copy = pltpu.make_async_copy(inten_hbm, inten_v, load_sem.at[3])
    here_copy = pltpu.make_async_copy(pos_hbm, pos, load_sem.at[0])
    here_copy.start()
    for j in range(per):
        for part in range(2):
            for q in range(loads):
                obj_copy(j, part, q).start()

    barrier = pltpu.get_barrier_semaphore()

    @pl.when(has_left)
    def _():
        pl.semaphore_signal(barrier, inc=1, device_id=left, device_id_type=MESH)

    @pl.when(has_right)
    def _():
        pl.semaphore_signal(barrier, inc=1, device_id=right, device_id_type=MESH)

    for o in range(1, ncut):
        peer = {"cuts": lax.rem(cut + o, ncut)}
        pl.semaphore_signal(barrier, inc=1, device_id=peer, device_id_type=MESH)
    peers = ncut - 1 + jnp.where(has_left, 1, 0) + jnp.where(has_right, 1, 0)
    here_copy.wait()
    pl.semaphore_wait(barrier, peers)

    pos_copy = pltpu.make_async_remote_copy(
        src_ref=pos, dst_ref=left_out, send_sem=pos_sem.at[0], recv_sem=pos_sem.at[1],
        device_id=right, device_id_type=MESH,
    )

    @pl.when(has_right)
    def _():
        pos_copy.start()

    lanes = lax.broadcasted_iota(jnp.int32, (height, cols), 1)
    glanes = lax.broadcasted_iota(jnp.int32, (half, cols), 1)
    first_lines = lax.broadcasted_iota(jnp.int32, (LANE_ROWS, cols), 0)

    def corner(slot):
        if slot < count:
            return left_out[slot, 0], left_out[slot, 1] - (tile - 1) * cols
        return pos[slot - count, 0], pos[slot - count, 1] - tile * cols

    def window_rows(row, j, part, k):
        base = lax.div(row, LANE_ROWS)
        part_groups = height // LANE_ROWS
        main = obj_v[j, part, pl.ds(base + k * part_groups, part_groups)].reshape(height, cols)
        if k > 0:
            return main
        wrapped = obj_v[j, part, base + width // LANE_ROWS]
        head = jnp.where(first_lines < row - base * LANE_ROWS, wrapped, main[:LANE_ROWS])
        return jnp.concatenate([head, main[LANE_ROWS:]], axis=0)

    def edge_copy(p, k):
        span = pl.ds(k * height, height)
        return pltpu.make_async_remote_copy(
            src_ref=edge_send.at[p, :, :, span, :], dst_ref=edge_recv.at[p, :, :, span, :],
            send_sem=e_ssem.at[p, k], recv_sem=e_rsem.at[p, k],
            device_id=right, device_id_type=MESH,
        )

    def inten_move(p):
        return pltpu.make_async_remote_copy(
            src_ref=inten_send.at[p], dst_ref=inten_b.at[p],
            send_sem=i_ssem.at[p], recv_sem=i_rsem.at[p],
            device_id=right, device_id_type=MESH,
        )

    def cross_copy(o, source, slot, k):
        span = pl.ds(k * height, height)
        part = win.at[slot, source, :, :, span, :]
        return pltpu.make_async_remote_copy(
            src_ref=part, dst_ref=part,
            send_sem=x_ssem.at[o - 1, slot, k], recv_sem=x_rsem.at[o - 1, slot, k],
            device_id={"cuts": lax.rem(cut + o, ncut)}, device_id_type=MESH,
        )

    def cross_start(slot, k):
        for o in range(1, ncut):
            if slot < count:
                cross_copy(o, cut, slot, k).start()
            else:
                to = lax.rem(cut + o, ncut)
                pl.when(to == (slot - count) % ncut)(lambda o=o: cross_copy(o, cut, slot, k).start())

    def return_copy(p, owner, j, b):
        span = pl.ds(b * half, half)
        return pltpu.make_async_remote_copy(
            src_ref=back_send.at[p, owner, j, :, span, :], dst_ref=got_out.at[p, j, :, span, :],
            send_sem=r_ssem.at[p, owner, j, b], recv_sem=r_rsem.at[p, j, b],
            device_id={"cuts": owner}, device_id_type=MESH,
        )

    def grad_copy(p, k):
        span = pl.ds(k * half, half)
        return pltpu.make_async_remote_copy(
            src_ref=grad_send.at[p, :, :, span, :], dst_ref=got_out.at[p, :, :, span, :],
            send_sem=g_ssem.at[p, k], recv_sem=g_rsem.at[p, k],
            device_id=left, device_id_type=MESH,
        )

    def merge(slot, k):
        row, col = corner(slot)
        span = pl.ds(k * height, height)
        for j in range(per):
            for part in range(2):
                cells = window_rows(row, j, part, k)
                if slot < count:
                    cells = jnp.where(
                        lanes < col, cells, edge_recv[slot, j, part, span, :].astype(F32)
                    )
                win[slot, cut, j, part, span, :] = cells.astype(BF16)

    for j in range(per):
        for part in range(2):
            for q in range(loads):
                obj_copy(j, part, q).wait()
            obj_v[j, part, groups] = jnp.zeros((LANE_ROWS, cols), F32)
    inten_copy.start()
    probe_copy.start()

    @pl.when(has_right)
    def _():
        for p in range(count):
            for k in range(chunks):
                for j in range(per):
                    for part in range(2):
                        edge_send[p, j, part, k * height : (k + 1) * height] = window_rows(
                            pos[p, 0], j, part, k
                        ).astype(BF16)
                edge_copy(p, k).start()

    @pl.when(last)
    def _():
        for slot in range(count, slots):
            for k in range(chunks):
                merge(slot, k)
                cross_start(slot, k)

    inten_copy.wait()
    inten_send[...] = inten_v[...].astype(BF16)

    @pl.when(has_right)
    def _():
        for p in range(count):
            inten_move(p).start()

    @pl.when(last)
    def _():
        inten_b[count:slots] = inten_send[...]

    tabs_copy.start()

    @pl.when(jnp.logical_not(has_left))
    def _():
        for p in range(count):
            for d in range(2):
                left_out[p, d] = 0
        own_out[0:count] = jnp.zeros((count, *own_out.shape[1:]), F32)

    @pl.when(has_left)
    def _():
        pos_copy.wait_recv()

    across = lax.broadcasted_iota(jnp.int32, (width, width), 1)
    down = lax.broadcasted_iota(jnp.int32, (width, width), 0)

    def illuminate(slot):
        row, col = corner(slot)
        shift = row - lax.div(row, LANE_ROWS) * LANE_ROWS
        source = across + shift
        move_rows = jnp.where(jnp.where(source >= width, source - width, source) == down, 1.0, 0.0)
        source = down + col
        move_cols = jnp.where(jnp.where(source >= width, source - width, source) == across, 1.0, 0.0)
        for part in range(2):
            rolled = dot(move_rows.astype(BF16), probe_v[part]).astype(BF16)
            psi[slot, 0, part] = dot(rolled, move_cols.astype(BF16)).astype(BF16)

    def prepare():
        probe_copy.wait()
        for slot in range(count):
            illuminate(slot)

        acc_out[...] = jnp.zeros_like(acc_out)
        for p in range(count):
            meta_out[2 * p] = jnp.full(meta_out.shape[1:], pos[p, 0], jnp.int32)
            meta_out[2 * p + 1] = jnp.full(meta_out.shape[1:], left_out[p, 0], jnp.int32)

        @pl.when(last)
        def _():
            for slot in range(count, slots):
                illuminate(slot)

    pl.when(even)(prepare)

    @pl.when(has_left)
    def _():
        for slot in range(count):
            for k in range(chunks):
                edge_copy(slot, k).wait_recv()
                merge(slot, k)
                if slot * chunks + k < early:
                    cross_start(slot, k)
                else:
                    pl.when(even)(lambda slot=slot, k=k: cross_start(slot, k))

    def go():
        pl.semaphore_signal(go_sem, inc=1, device_id=right, device_id_type=MESH)

    leads = jnp.logical_and(even, has_right)
    pl.when(jnp.logical_and(leads, jnp.logical_not(has_left)))(go)

    pl.when(odd)(prepare)

    tabs_copy.wait()

    @pl.when(odd)
    def _():
        pl.semaphore_wait(go_sem, 1)
        for i in range(early, count * chunks):
            cross_start(i // chunks, i % chunks)


    def arrive(slot, owner):
        @pl.when(owner != cut)
        def _():
            o = lax.rem(cut - owner + ncut, ncut)
            for k in range(chunks):
                cross_copy(o, owner, slot, k).wait_recv()

    def stage(first, second, stacked, point):
        sides = []
        for b in range(gchunks):
            up, down = b * half, width + b * half
            rows_of = jnp.concatenate(
                [tabs_v[first, up : up + half], tabs_v[first, down : down + half]], axis=0
            )
            inner = dot(rows_of, stacked).astype(BF16)
            sides.append(jnp.concatenate([inner[:half], inner[half:]], axis=1))
        for b in range(gchunks):
            out = dot(sides[b], tabs_v[second])
            point(b, out[:, :width], out[:, width:])

    def put(ref, b, re, im):
        ref[pl.ds(b * half, half)] = re.astype(BF16)
        ref[pl.ds(width + b * half, half)] = im.astype(BF16)

    def transmission(slot, s, span):
        owner, j = s // per, lax.rem(s, per)
        return (
            1.0 + win[slot, owner, j, 0, span].astype(F32),
            win[slot, owner, j, 1, span].astype(F32),
        )

    def incident(slot, s, span):
        return psi[slot, s, 0, span].astype(F32), psi[slot, s, 1, span].astype(F32)

    def leave(slot, s):
        for b in range(gchunks):
            span = pl.ds(b * half, half)
            t_re, t_im = transmission(slot, s, span)
            p_re, p_im = incident(slot, s, span)
            put(wave, b, p_re * t_re - p_im * t_im, p_re * t_im + p_im * t_re)

    def adjoint_slice(slot, s, first, second, source):
        owner, j = s // per, lax.rem(s, per)
        foreign = slot < count
        p = jnp.where(foreign, slot, slot - count)
        col = jnp.where(
            foreign, left_out[p, 1] - (tile - 1) * cols, pos[p, 1] - tile * cols
        )
        low, high = jnp.where(foreign, 0, col), jnp.where(foreign, col, cols)

        @pl.when(jnp.logical_and(foreign, owner == cut))
        def _():
            def gradient(b, m_re, m_im):
                span = pl.ds(b * half, half)
                p_re, p_im = incident(slot, s, span)
                g = (p_re * m_re + p_im * m_im, p_re * m_im - p_im * m_re)
                mine = jnp.logical_and(glanes >= low, glanes < high)
                for part in range(2):
                    own_out[slot, j, part, span, :] = jnp.where(mine, g[part], 0.0)
                    grad_send[slot, j, part, span, :] = jnp.where(mine, 0.0, g[part]).astype(BF16)
                if per == 1:

                    grad_copy(slot, b).start()

            stage(first, second, source[...], gradient)

        @pl.when(jnp.logical_not(foreign))
        def _():
            def alone(b, m_re, m_im):
                span = pl.ds(b * half, half)
                p_re, p_im = incident(slot, s, span)
                mine = jnp.logical_and(glanes >= low, glanes < high)
                g = (p_re * m_re + p_im * m_im, p_re * m_im - p_im * m_re)
                for part in range(2):
                    back_send[p, owner, j, part, span, :] = jnp.where(mine, g[part], 0.0).astype(
                        BF16
                    )

                @pl.when(owner == cut)
                def _():
                    got_out[p, j, :, span, :] = back_send[p, owner, j, :, span, :]

                @pl.when(owner != cut)
                def _():
                    return_copy(p, owner, j, b).start()

            stage(first, second, source[...], alone)

        @pl.when(s > jnp.where(foreign, cut * per, 0))
        def _():
            def back(b, m_re, m_im):
                t_re, t_im = transmission(slot, s, pl.ds(b * half, half))
                put(wave, b, t_re * m_re + t_im * m_im, t_re * m_im - t_im * m_re)

            stage(first, second, source[...], back)

    def one_probe(slot):
        def forward(s):
            arrive(slot, s // per)
            leave(slot, s)

            def keep_wave(b, re, im):
                psi[slot, s + 1, 0, pl.ds(b * half, half)] = re.astype(BF16)
                psi[slot, s + 1, 1, pl.ds(b * half, half)] = im.astype(BF16)

            stage(0, 1, wave[...], keep_wave)

        def backward(i):
            s = total - 2 - i

            @pl.when(jnp.logical_or(slot >= count, s >= cut * per))
            def _():
                adjoint_slice(slot, s, 1, 0, wave)

        if per == 1:
            repeat(total - 1, forward)
            arrive(slot, total - 1)
        else:
            for s in range(ncut):
                arrive(slot, s)
            for s in range(total - 1):
                leave(slot, s)

                def keep_wave(b, re, im, s=s):
                    psi[slot, s + 1, 0, pl.ds(b * half, half)] = re.astype(BF16)
                    psi[slot, s + 1, 1, pl.ds(b * half, half)] = im.astype(BF16)

                stage(0, 1, wave[...], keep_wave)
        leave(slot, total - 1)

        for p in range(count):
            pl.when(slot == p)(lambda p=p: inten_move(p).wait_recv())

        def misfit(b, re, im):
            gap = re * re + im * im - inten_b[slot, pl.ds(b * half, half)].astype(F32)
            put(lam, b, gap * re, gap * im)

        pl.when(jnp.logical_and(leads, slot == 0))(go)
        stage(2, 3, wave[...], misfit)
        adjoint_slice(slot, total - 1, 3, 2, lam)
        repeat(total - 1, backward)
        if per > 1:
            for b in range(gchunks):

                @pl.when(slot < count)
                def _():
                    grad_copy(slot, b).start()

    def turn(i, _):
        final = jnp.where(i < count, i + count, i - count)
        slot = jnp.where(has_right, i, final)
        here = lax.rem(jnp.maximum(slot - count, 0), ncut) == cut
        pl.when(jnp.logical_or(slot < count, here))(lambda: one_probe(slot))
        return 0

    turns = jnp.where(has_left, count, 0) + jnp.where(has_right, 0, count)
    lax.fori_loop(0, turns, turn, 0)

    def cross_drain(slot):
        for k in range(chunks):
            for o in range(1, ncut):
                cross_copy(o, cut, slot, k).wait_send()

    @pl.when(last)
    def _():
        for p in range(count):
            host = p % ncut
            for o in range(1, ncut):

                @pl.when(lax.rem(cut + o, ncut) == host)
                def _():
                    for k in range(chunks):
                        cross_copy(o, cut, count + p, k).wait_send()

            for owner in range(ncut):
                for j in range(per):
                    for b in range(gchunks):
                        if owner != host:
                            pl.when(cut == host)(
                                lambda: return_copy(p, owner, j, b).wait_send()
                            )
                            pl.when(cut == owner)(
                                lambda: return_copy(p, host, j, b).wait_recv()
                            )

    @pl.when(has_right)
    def _():
        pos_copy.wait_send()
        for p in range(count):
            inten_move(p).wait_send()
            for k in range(chunks):
                edge_copy(p, k).wait_send()
        for p in range(count):
            for k in range(gchunks):
                grad_copy(p, k).wait_recv()

    @pl.when(has_left)
    def _():
        for slot in range(count):
            for k in range(chunks):

                for o in range(1, ncut):
                    cross_copy(o, cut, slot, k).wait_send()

            for k in range(gchunks):
                grad_copy(slot, k).wait_send()


def place_kernel(own, got, meta, _, out_hbm, out_v, sem):
    per, _, rows, cols = out_v.shape
    count, width = got.shape[0], got.shape[3]
    iota = lax.broadcasted_iota(jnp.int32, (LANE_ROWS, cols), 0)

    step = width // 4

    def add(source, row, p, j, part):
        base = row // LANE_ROWS * LANE_ROWS
        shift = row - base
        after = pl.multiple_of(jnp.minimum(base + width, rows - LANE_ROWS), LANE_ROWS)
        head = source[p, j, part, :16].astype(F32)[:LANE_ROWS]
        for r in range(4):
            cells = source[p, j, part, r * step : (r + 1) * step].astype(F32)
            if r == 0:
                cells = jnp.concatenate(
                    [jnp.where(iota >= shift, cells[:LANE_ROWS], 0.0), cells[LANE_ROWS:]], axis=0
                )
            at = pl.ds(pl.multiple_of(base + r * step, LANE_ROWS), step)
            out_v[j, part, at, :] += cells
        out_v[j, part, pl.ds(after, LANE_ROWS), :] += jnp.where(iota < shift, head, 0.0)

    blocks = sem.shape[-1]
    span = rows // blocks
    corners = [jnp.max(meta[i]) for i in range(2 * count)]

    def touched(b):
        hit = False
        for row in corners:
            near = jnp.logical_and(row < (b + 1) * span, row + width + LANE_ROWS > b * span)
            hit = jnp.logical_or(hit, near)
        return hit

    def block_copy(j, part, b):
        at = pl.ds(b * span, span)
        return pltpu.make_async_copy(
            out_v.at[j, part, at, :], out_hbm.at[j, part, at, :], sem.at[j, part, b]
        )

    busy = [touched(b) for b in range(blocks)]
    for j in range(per):
        for part in range(2):
            for b in range(blocks):
                pl.when(jnp.logical_not(busy[b]))(lambda: block_copy(j, part, b).start())
    for j in range(per):
        for part in range(2):
            for p in range(count):
                add(own, corners[2 * p + 1], p, j, part)
                add(got, corners[2 * p], p, j, part)
            for b in range(blocks):
                pl.when(busy[b])(lambda: block_copy(j, part, b).start())
    for j in range(per):
        for part in range(2):
            for b in range(blocks):
                block_copy(j, part, b).wait()


def per_device(tables, object_delta, probe_wave, intensity, positions):
    per, _, rows, cols = object_delta.shape
    count, width = intensity.shape[0], intensity.shape[1]
    ncut = lax.axis_size("cuts")
    chunks, gchunks, loads, early = 4, 2, 4, 2
    anywhere = pl.BlockSpec(memory_space=pl.ANY)
    vmem = pl.BlockSpec(memory_space=pltpu.VMEM)
    dma = pltpu.SemaphoreType.DMA
    piece = (count, per, 2, width, cols)
    others = max(ncut - 1, 1)
    slots = 2 * count
    own, got, meta, acc = pl.pallas_call(
        functools.partial(exchange_kernel, chunks=chunks, gchunks=gchunks, early=early),
        out_shape=(
            pltpu.VMEM((slots, *piece[1:]), F32),
            pltpu.VMEM(piece, BF16),
            pltpu.VMEM((2 * count, LANE_ROWS, 128), jnp.int32),
            pltpu.VMEM(object_delta.shape, F32),
        ),
        in_specs=[anywhere] * 5,
        out_specs=(vmem, vmem, vmem, vmem),
        scratch_shapes=[
            pltpu.SMEM(positions.shape, positions.dtype),
            pltpu.SMEM(positions.shape, positions.dtype),
            pltpu.VMEM((per, 2, rows // LANE_ROWS + 1, LANE_ROWS, cols), F32),
            pltpu.VMEM(probe_wave.shape, BF16),
            pltpu.VMEM(intensity.shape, F32),
            pltpu.VMEM(tables.shape, BF16),
            pltpu.VMEM(piece, BF16),
            pltpu.VMEM(piece, BF16),
            pltpu.VMEM(intensity.shape, BF16),
            pltpu.VMEM((slots, width, cols), BF16),
            pltpu.VMEM((slots, ncut, per, 2, width, cols), BF16),
            pltpu.VMEM((slots, ncut * per, 2, width, cols), BF16),
            pltpu.VMEM((2 * width, cols), BF16),
            pltpu.VMEM((2 * width, cols), BF16),
            pltpu.VMEM((slots, *piece[1:]), BF16),
            pltpu.VMEM((count, ncut, *piece[1:]), BF16),
            dma((per, 2, loads)),
            dma((4,)),
            dma((2,)),
            dma((count, chunks)),
            dma((count, chunks)),
            dma((others, slots, chunks)),
            dma((others, slots, chunks)),
            dma((count, gchunks)),
            dma((count, gchunks)),
            dma((count,)),
            dma((count,)),
            dma((count, ncut, per, gchunks)),
            dma((count, per, gchunks)),
            pltpu.SemaphoreType.REGULAR,
        ],
        compiler_params=pltpu.CompilerParams(
            collective_id=0, has_side_effects=True, vmem_limit_bytes=56 << 20
        ),
        name="exchange",
    )(
        object_delta.reshape(per, 2, rows // LANE_ROWS, LANE_ROWS, cols),
        probe_wave, intensity, positions, tables,
    )
    own = pltpu.with_memory_space_constraint(own, pltpu.VMEM)
    got = pltpu.with_memory_space_constraint(got, pltpu.VMEM)
    acc = pltpu.with_memory_space_constraint(acc, pltpu.VMEM)
    meta = pltpu.with_memory_space_constraint(meta, pltpu.VMEM)
    placed, _ = pl.pallas_call(
        place_kernel,
        out_shape=(
            jax.ShapeDtypeStruct(object_delta.shape, F32),
            pltpu.VMEM(object_delta.shape, F32),
        ),
        in_specs=[vmem, vmem, vmem, vmem],
        out_specs=(anywhere, vmem),
        scratch_shapes=[dma((per, 2, 4))],
        compiler_params=pltpu.CompilerParams(vmem_limit_bytes=56 << 20),
        input_output_aliases={3: 1},
        name="place",
    )(own, got, meta, acc)
    return placed


def solution(mesh):
    def whole(object_delta, probe_wave, intensity, positions):
        tables = jnp.asarray(make_tables(probe_wave.shape[-1]))
        return jax.shard_map(
            per_device,
            mesh=mesh,
            in_specs=(
                P(),
                P("cuts", None, None, "tile"),
                P(),
                P("tile", None, None),
                P("tile", None),
            ),
            out_specs=P("cuts", None, None, "tile"),
            check_vma=False,
        )(tables, object_delta, probe_wave, intensity, positions)

    return whole
```

```python
import functools
import math

import jax
import jax.numpy as jnp
import numpy as np
from jax import lax
from jax.experimental import pallas as pl
from jax.experimental.pallas import tpu as pltpu
from jax.sharding import PartitionSpec as P

F32 = jnp.float32
BF16 = jnp.bfloat16
MESH = pl.DeviceIdType.MESH
LANE_ROWS = 8


def make_tables(width):
    counter = np.arange(width)
    phase = (counter[:, None] * counter[None, :] % width) * (2.0 * math.pi / width)
    four = np.exp(-1j * phase) / math.sqrt(width)
    signed = np.where(counter < width // 2, counter, counter - width).astype(np.float64)
    kernel = np.exp(-2j * math.pi / width * signed * signed)
    prop = np.conj(four) @ (kernel[:, None] * four)
    prop = 0.5 * (prop + prop.T)

    def block(table):
        re, im = table.real, table.imag
        return np.block([[re, -im], [im, re]])

    big = [block(prop), block(prop).T, block(four), block(four).T]
    return np.stack(big).astype(np.float32).astype(jnp.bfloat16)


def dot(a, b):
    return jnp.dot(a, b, preferred_element_type=F32)


def repeat(count, body):
    if count == 1:
        body(0)
    elif count > 1:
        lax.fori_loop(0, count, lambda i, _: (body(i), 0)[1], 0)


def exchange_kernel(
    obj_hbm, probe_hbm, inten_hbm, pos_hbm, tabs_hbm,
    own_out, got_out, meta_out, acc_out,
    pos, left_out, obj_v, probe_v, inten_v, tabs_v, edge_send, edge_recv, inten_send, inten_b,
    win, psi, wave, lam, grad_send, back_send,
    obj_sem, load_sem, pos_sem, e_ssem, e_rsem, x_ssem, x_rsem, g_ssem, g_rsem, i_ssem, i_rsem, r_ssem, r_rsem, go_sem,
    *, chunks, gchunks, early,
):
    cut, tile = lax.axis_index("cuts"), lax.axis_index("tile")
    ncut, ntile = lax.axis_size("cuts"), lax.axis_size("tile")
    per, cols = obj_v.shape[0], obj_v.shape[-1]
    groups = obj_hbm.shape[2]
    count, width = inten_v.shape[0], inten_v.shape[1]
    slots = 2 * count
    total = ncut * per
    height = width // chunks
    half = width // gchunks
    has_left, has_right = tile > 0, tile < ntile - 1
    last = jnp.logical_not(has_right)
    odd = lax.rem(tile, 2) == 1
    even = jnp.logical_not(odd)
    left, right = {"tile": tile - 1}, {"tile": tile + 1}
    loads = obj_sem.shape[-1]
    load_groups = groups // loads

    def obj_copy(j, part, q):
        span = pl.ds(q * load_groups, load_groups)
        return pltpu.make_async_copy(
            obj_hbm.at[j, part, span], obj_v.at[j, part, span], obj_sem.at[j, part, q]
        )

    probe_copy = pltpu.make_async_copy(probe_hbm, probe_v, load_sem.at[1])
    tabs_copy = pltpu.make_async_copy(tabs_hbm, tabs_v, load_sem.at[2])
    inten_copy = pltpu.make_async_copy(inten_hbm, inten_v, load_sem.at[3])
    here_copy = pltpu.make_async_copy(pos_hbm, pos, load_sem.at[0])
    here_copy.start()
    for j in range(per):
        for part in range(2):
            for q in range(loads):
                obj_copy(j, part, q).start()

    barrier = pltpu.get_barrier_semaphore()

    @pl.when(has_left)
    def _():
        pl.semaphore_signal(barrier, inc=1, device_id=left, device_id_type=MESH)

    @pl.when(has_right)
    def _():
        pl.semaphore_signal(barrier, inc=1, device_id=right, device_id_type=MESH)

    for o in range(1, ncut):
        peer = {"cuts": lax.rem(cut + o, ncut)}
        pl.semaphore_signal(barrier, inc=1, device_id=peer, device_id_type=MESH)
    peers = ncut - 1 + jnp.where(has_left, 1, 0) + jnp.where(has_right, 1, 0)
    here_copy.wait()
    pl.semaphore_wait(barrier, peers)

    pos_copy = pltpu.make_async_remote_copy(
        src_ref=pos, dst_ref=left_out, send_sem=pos_sem.at[0], recv_sem=pos_sem.at[1],
        device_id=right, device_id_type=MESH,
    )

    @pl.when(has_right)
    def _():
        pos_copy.start()

    lanes = lax.broadcasted_iota(jnp.int32, (height, cols), 1)
    glanes = lax.broadcasted_iota(jnp.int32, (half, cols), 1)
    first_lines = lax.broadcasted_iota(jnp.int32, (LANE_ROWS, cols), 0)

    def corner(slot):
        if slot < count:
            return left_out[slot, 0], left_out[slot, 1] - (tile - 1) * cols
        return pos[slot - count, 0], pos[slot - count, 1] - tile * cols

    def window_rows(row, j, part, k):
        base = lax.div(row, LANE_ROWS)
        part_groups = height // LANE_ROWS
        main = obj_v[j, part, pl.ds(base + k * part_groups, part_groups)].reshape(height, cols)
        if k > 0:
            return main
        wrapped = obj_v[j, part, base + width // LANE_ROWS]
        head = jnp.where(first_lines < row - base * LANE_ROWS, wrapped, main[:LANE_ROWS])
        return jnp.concatenate([head, main[LANE_ROWS:]], axis=0)

    def edge_copy(p, k):
        span = pl.ds(k * height, height)
        return pltpu.make_async_remote_copy(
            src_ref=edge_send.at[p, :, :, span, :], dst_ref=edge_recv.at[p, :, :, span, :],
            send_sem=e_ssem.at[p, k], recv_sem=e_rsem.at[p, k],
            device_id=right, device_id_type=MESH,
        )

    def inten_move(p):
        return pltpu.make_async_remote_copy(
            src_ref=inten_send.at[p], dst_ref=inten_b.at[p],
            send_sem=i_ssem.at[p], recv_sem=i_rsem.at[p],
            device_id=right, device_id_type=MESH,
        )

    def cross_copy(o, source, slot, k):
        span = pl.ds(k * height, height)
        part = win.at[slot, source, :, :, span, :]
        return pltpu.make_async_remote_copy(
            src_ref=part, dst_ref=part,
            send_sem=x_ssem.at[o - 1, slot, k], recv_sem=x_rsem.at[o - 1, slot, k],
            device_id={"cuts": lax.rem(cut + o, ncut)}, device_id_type=MESH,
        )

    def cross_start(slot, k):
        for o in range(1, ncut):
            if slot < count:
                cross_copy(o, cut, slot, k).start()
            else:
                to = lax.rem(cut + o, ncut)
                pl.when(to == (slot - count) % ncut)(lambda o=o: cross_copy(o, cut, slot, k).start())

    def return_copy(p, owner, j, b):
        span = pl.ds(b * half, half)
        return pltpu.make_async_remote_copy(
            src_ref=back_send.at[p, owner, j, :, span, :], dst_ref=got_out.at[p, j, :, span, :],
            send_sem=r_ssem.at[p, owner, j, b], recv_sem=r_rsem.at[p, j, b],
            device_id={"cuts": owner}, device_id_type=MESH,
        )

    def grad_copy(p, k):
        span = pl.ds(k * half, half)
        return pltpu.make_async_remote_copy(
            src_ref=grad_send.at[p, :, :, span, :], dst_ref=got_out.at[p, :, :, span, :],
            send_sem=g_ssem.at[p, k], recv_sem=g_rsem.at[p, k],
            device_id=left, device_id_type=MESH,
        )

    def merge(slot, k):
        row, col = corner(slot)
        span = pl.ds(k * height, height)
        for j in range(per):
            for part in range(2):
                cells = window_rows(row, j, part, k)
                if slot < count:
                    cells = jnp.where(
                        lanes < col, cells, edge_recv[slot, j, part, span, :].astype(F32)
                    )
                win[slot, cut, j, part, span, :] = cells.astype(BF16)

    for j in range(per):
        for part in range(2):
            for q in range(loads):
                obj_copy(j, part, q).wait()
            obj_v[j, part, groups] = jnp.zeros((LANE_ROWS, cols), F32)
    inten_copy.start()
    probe_copy.start()

    @pl.when(has_right)
    def _():
        for p in range(count):
            for k in range(chunks):
                for j in range(per):
                    for part in range(2):
                        edge_send[p, j, part, k * height : (k + 1) * height] = window_rows(
                            pos[p, 0], j, part, k
                        ).astype(BF16)
                edge_copy(p, k).start()

    @pl.when(last)
    def _():
        for slot in range(count, slots):
            for k in range(chunks):
                merge(slot, k)
                cross_start(slot, k)

    inten_copy.wait()
    inten_send[...] = inten_v[...].astype(BF16)

    @pl.when(has_right)
    def _():
        for p in range(count):
            inten_move(p).start()

    @pl.when(last)
    def _():
        inten_b[count:slots] = inten_send[...]

    tabs_copy.start()

    @pl.when(jnp.logical_not(has_left))
    def _():
        for p in range(count):
            for d in range(2):
                left_out[p, d] = 0
        own_out[0:count] = jnp.zeros((count, *own_out.shape[1:]), F32)

    @pl.when(has_left)
    def _():
        pos_copy.wait_recv()

    across = lax.broadcasted_iota(jnp.int32, (width, width), 1)
    down = lax.broadcasted_iota(jnp.int32, (width, width), 0)

    def illuminate(slot):
        row, col = corner(slot)
        shift = row - lax.div(row, LANE_ROWS) * LANE_ROWS
        source = across + shift
        move_rows = jnp.where(jnp.where(source >= width, source - width, source) == down, 1.0, 0.0)
        source = down + col
        move_cols = jnp.where(jnp.where(source >= width, source - width, source) == across, 1.0, 0.0)
        for part in range(2):
            rolled = dot(move_rows.astype(BF16), probe_v[part]).astype(BF16)
            psi[slot, 0, part] = dot(rolled, move_cols.astype(BF16)).astype(BF16)

    def prepare():
        probe_copy.wait()
        for slot in range(count):
            illuminate(slot)

        acc_out[...] = jnp.zeros_like(acc_out)
        for p in range(count):
            meta_out[2 * p] = jnp.full(meta_out.shape[1:], pos[p, 0], jnp.int32)
            meta_out[2 * p + 1] = jnp.full(meta_out.shape[1:], left_out[p, 0], jnp.int32)

        @pl.when(last)
        def _():
            for slot in range(count, slots):
                illuminate(slot)

    pl.when(even)(prepare)

    @pl.when(has_left)
    def _():
        for slot in range(count):
            for k in range(chunks):
                edge_copy(slot, k).wait_recv()
                merge(slot, k)
                if slot * chunks + k < early:
                    cross_start(slot, k)
                else:
                    pl.when(even)(lambda slot=slot, k=k: cross_start(slot, k))

    def go():
        pl.semaphore_signal(go_sem, inc=1, device_id=right, device_id_type=MESH)

    leads = jnp.logical_and(even, has_right)
    pl.when(jnp.logical_and(leads, jnp.logical_not(has_left)))(go)

    pl.when(odd)(prepare)

    tabs_copy.wait()

    @pl.when(odd)
    def _():
        pl.semaphore_wait(go_sem, 1)
        for i in range(early, count * chunks):
            cross_start(i // chunks, i % chunks)


    def arrive(slot, owner):
        @pl.when(owner != cut)
        def _():
            o = lax.rem(cut - owner + ncut, ncut)
            for k in range(chunks):
                cross_copy(o, owner, slot, k).wait_recv()

    def stage(first, second, stacked, point):
        sides = []
        for b in range(gchunks):
            up, down = b * half, width + b * half
            rows_of = jnp.concatenate(
                [tabs_v[first, up : up + half], tabs_v[first, down : down + half]], axis=0
            )
            inner = dot(rows_of, stacked).astype(BF16)
            sides.append(jnp.concatenate([inner[:half], inner[half:]], axis=1))
        for b in range(gchunks):
            out = dot(sides[b], tabs_v[second])
            point(b, out[:, :width], out[:, width:])

    def put(ref, b, re, im):
        ref[pl.ds(b * half, half)] = re.astype(BF16)
        ref[pl.ds(width + b * half, half)] = im.astype(BF16)

    def transmission(slot, s, span):
        owner, j = s // per, lax.rem(s, per)
        return (
            1.0 + win[slot, owner, j, 0, span].astype(F32),
            win[slot, owner, j, 1, span].astype(F32),
        )

    def incident(slot, s, span):
        return psi[slot, s, 0, span].astype(F32), psi[slot, s, 1, span].astype(F32)

    def leave(slot, s):
        for b in range(gchunks):
            span = pl.ds(b * half, half)
            t_re, t_im = transmission(slot, s, span)
            p_re, p_im = incident(slot, s, span)
            put(wave, b, p_re * t_re - p_im * t_im, p_re * t_im + p_im * t_re)

    def adjoint_slice(slot, s, first, second, source):
        owner, j = s // per, lax.rem(s, per)
        foreign = slot < count
        p = jnp.where(foreign, slot, slot - count)
        col = jnp.where(
            foreign, left_out[p, 1] - (tile - 1) * cols, pos[p, 1] - tile * cols
        )
        low, high = jnp.where(foreign, 0, col), jnp.where(foreign, col, cols)

        @pl.when(jnp.logical_and(foreign, owner == cut))
        def _():
            def gradient(b, m_re, m_im):
                span = pl.ds(b * half, half)
                p_re, p_im = incident(slot, s, span)
                g = (p_re * m_re + p_im * m_im, p_re * m_im - p_im * m_re)
                mine = jnp.logical_and(glanes >= low, glanes < high)
                for part in range(2):
                    own_out[slot, j, part, span, :] = jnp.where(mine, g[part], 0.0)
                    grad_send[slot, j, part, span, :] = jnp.where(mine, 0.0, g[part]).astype(BF16)
                if per == 1:

                    grad_copy(slot, b).start()

            stage(first, second, source[...], gradient)

        @pl.when(jnp.logical_not(foreign))
        def _():
            def alone(b, m_re, m_im):
                span = pl.ds(b * half, half)
                p_re, p_im = incident(slot, s, span)
                mine = jnp.logical_and(glanes >= low, glanes < high)
                g = (p_re * m_re + p_im * m_im, p_re * m_im - p_im * m_re)
                for part in range(2):
                    back_send[p, owner, j, part, span, :] = jnp.where(mine, g[part], 0.0).astype(
                        BF16
                    )

                @pl.when(owner == cut)
                def _():
                    got_out[p, j, :, span, :] = back_send[p, owner, j, :, span, :]

                @pl.when(owner != cut)
                def _():
                    return_copy(p, owner, j, b).start()

            stage(first, second, source[...], alone)

        @pl.when(s > jnp.where(foreign, cut * per, 0))
        def _():
            def back(b, m_re, m_im):
                t_re, t_im = transmission(slot, s, pl.ds(b * half, half))
                put(wave, b, t_re * m_re + t_im * m_im, t_re * m_im - t_im * m_re)

            stage(first, second, source[...], back)

    def one_probe(slot):
        def forward(s):
            arrive(slot, s // per)
            leave(slot, s)

            def keep_wave(b, re, im):
                psi[slot, s + 1, 0, pl.ds(b * half, half)] = re.astype(BF16)
                psi[slot, s + 1, 1, pl.ds(b * half, half)] = im.astype(BF16)

            stage(0, 1, wave[...], keep_wave)

        def backward(i):
            s = total - 2 - i

            @pl.when(jnp.logical_or(slot >= count, s >= cut * per))
            def _():
                adjoint_slice(slot, s, 1, 0, wave)

        if per == 1:
            repeat(total - 1, forward)
            arrive(slot, total - 1)
        else:
            for s in range(ncut):
                arrive(slot, s)
            for s in range(total - 1):
                leave(slot, s)

                def keep_wave(b, re, im, s=s):
                    psi[slot, s + 1, 0, pl.ds(b * half, half)] = re.astype(BF16)
                    psi[slot, s + 1, 1, pl.ds(b * half, half)] = im.astype(BF16)

                stage(0, 1, wave[...], keep_wave)
        pl.when(jnp.logical_and(leads, slot == 0))(go)
        leave(slot, total - 1)

        for p in range(count):
            pl.when(slot == p)(lambda p=p: inten_move(p).wait_recv())

        def misfit(b, re, im):
            gap = re * re + im * im - inten_b[slot, pl.ds(b * half, half)].astype(F32)
            put(lam, b, gap * re, gap * im)

        stage(2, 3, wave[...], misfit)
        adjoint_slice(slot, total - 1, 3, 2, lam)
        repeat(total - 1, backward)
        if per > 1:
            for b in range(gchunks):

                @pl.when(slot < count)
                def _():
                    grad_copy(slot, b).start()

    def turn(i, _):
        final = jnp.where(i < count, i + count, i - count)
        slot = jnp.where(has_right, i, final)
        here = lax.rem(jnp.maximum(slot - count, 0), ncut) == cut
        pl.when(jnp.logical_or(slot < count, here))(lambda: one_probe(slot))
        return 0

    turns = jnp.where(has_left, count, 0) + jnp.where(has_right, 0, count)
    lax.fori_loop(0, turns, turn, 0)

    def cross_drain(slot):
        for k in range(chunks):
            for o in range(1, ncut):
                cross_copy(o, cut, slot, k).wait_send()

    @pl.when(last)
    def _():
        for p in range(count):
            host = p % ncut
            for o in range(1, ncut):

                @pl.when(lax.rem(cut + o, ncut) == host)
                def _():
                    for k in range(chunks):
                        cross_copy(o, cut, count + p, k).wait_send()

            for owner in range(ncut):
                for j in range(per):
                    for b in range(gchunks):
                        if owner != host:
                            pl.when(cut == host)(
                                lambda: return_copy(p, owner, j, b).wait_send()
                            )
                            pl.when(cut == owner)(
                                lambda: return_copy(p, host, j, b).wait_recv()
                            )

    @pl.when(has_right)
    def _():
        pos_copy.wait_send()
        for p in range(count):
            inten_move(p).wait_send()
            for k in range(chunks):
                edge_copy(p, k).wait_send()
        for p in range(count):
            for k in range(gchunks):
                grad_copy(p, k).wait_recv()

    @pl.when(has_left)
    def _():
        for slot in range(count):
            for k in range(chunks):

                for o in range(1, ncut):
                    cross_copy(o, cut, slot, k).wait_send()

            for k in range(gchunks):
                grad_copy(slot, k).wait_send()


def place_kernel(own, got, meta, _, out_hbm, out_v, sem):
    per, _, rows, cols = out_v.shape
    count, width = got.shape[0], got.shape[3]
    iota = lax.broadcasted_iota(jnp.int32, (LANE_ROWS, cols), 0)

    step = width // 4

    def add(source, row, p, j, part):
        base = row // LANE_ROWS * LANE_ROWS
        shift = row - base
        after = pl.multiple_of(jnp.minimum(base + width, rows - LANE_ROWS), LANE_ROWS)
        head = source[p, j, part, :16].astype(F32)[:LANE_ROWS]
        for r in range(4):
            cells = source[p, j, part, r * step : (r + 1) * step].astype(F32)
            if r == 0:
                cells = jnp.concatenate(
                    [jnp.where(iota >= shift, cells[:LANE_ROWS], 0.0), cells[LANE_ROWS:]], axis=0
                )
            at = pl.ds(pl.multiple_of(base + r * step, LANE_ROWS), step)
            out_v[j, part, at, :] += cells
        out_v[j, part, pl.ds(after, LANE_ROWS), :] += jnp.where(iota < shift, head, 0.0)

    blocks = sem.shape[-1]
    span = rows // blocks
    corners = [jnp.max(meta[i]) for i in range(2 * count)]

    def touched(b):
        hit = False
        for row in corners:
            near = jnp.logical_and(row < (b + 1) * span, row + width + LANE_ROWS > b * span)
            hit = jnp.logical_or(hit, near)
        return hit

    def block_copy(j, part, b):
        at = pl.ds(b * span, span)
        return pltpu.make_async_copy(
            out_v.at[j, part, at, :], out_hbm.at[j, part, at, :], sem.at[j, part, b]
        )

    busy = [touched(b) for b in range(blocks)]
    for j in range(per):
        for part in range(2):
            for b in range(blocks):
                pl.when(jnp.logical_not(busy[b]))(lambda: block_copy(j, part, b).start())
    for j in range(per):
        for part in range(2):
            for p in range(count):
                add(own, corners[2 * p + 1], p, j, part)
                add(got, corners[2 * p], p, j, part)
            for b in range(blocks):
                pl.when(busy[b])(lambda: block_copy(j, part, b).start())
    for j in range(per):
        for part in range(2):
            for b in range(blocks):
                block_copy(j, part, b).wait()


def per_device(tables, object_delta, probe_wave, intensity, positions):
    per, _, rows, cols = object_delta.shape
    count, width = intensity.shape[0], intensity.shape[1]
    ncut = lax.axis_size("cuts")
    chunks, gchunks, loads, early = 4, 2, 4, 2
    anywhere = pl.BlockSpec(memory_space=pl.ANY)
    vmem = pl.BlockSpec(memory_space=pltpu.VMEM)
    dma = pltpu.SemaphoreType.DMA
    piece = (count, per, 2, width, cols)
    others = max(ncut - 1, 1)
    slots = 2 * count
    own, got, meta, acc = pl.pallas_call(
        functools.partial(exchange_kernel, chunks=chunks, gchunks=gchunks, early=early),
        out_shape=(
            pltpu.VMEM((slots, *piece[1:]), F32),
            pltpu.VMEM(piece, BF16),
            pltpu.VMEM((2 * count, LANE_ROWS, 128), jnp.int32),
            pltpu.VMEM(object_delta.shape, F32),
        ),
        in_specs=[anywhere] * 5,
        out_specs=(vmem, vmem, vmem, vmem),
        scratch_shapes=[
            pltpu.SMEM(positions.shape, positions.dtype),
            pltpu.SMEM(positions.shape, positions.dtype),
            pltpu.VMEM((per, 2, rows // LANE_ROWS + 1, LANE_ROWS, cols), F32),
            pltpu.VMEM(probe_wave.shape, BF16),
            pltpu.VMEM(intensity.shape, F32),
            pltpu.VMEM(tables.shape, BF16),
            pltpu.VMEM(piece, BF16),
            pltpu.VMEM(piece, BF16),
            pltpu.VMEM(intensity.shape, BF16),
            pltpu.VMEM((slots, width, cols), BF16),
            pltpu.VMEM((slots, ncut, per, 2, width, cols), BF16),
            pltpu.VMEM((slots, ncut * per, 2, width, cols), BF16),
            pltpu.VMEM((2 * width, cols), BF16),
            pltpu.VMEM((2 * width, cols), BF16),
            pltpu.VMEM((slots, *piece[1:]), BF16),
            pltpu.VMEM((count, ncut, *piece[1:]), BF16),
            dma((per, 2, loads)),
            dma((4,)),
            dma((2,)),
            dma((count, chunks)),
            dma((count, chunks)),
            dma((others, slots, chunks)),
            dma((others, slots, chunks)),
            dma((count, gchunks)),
            dma((count, gchunks)),
            dma((count,)),
            dma((count,)),
            dma((count, ncut, per, gchunks)),
            dma((count, per, gchunks)),
            pltpu.SemaphoreType.REGULAR,
        ],
        compiler_params=pltpu.CompilerParams(
            collective_id=0, has_side_effects=True, vmem_limit_bytes=56 << 20
        ),
        name="exchange",
    )(
        object_delta.reshape(per, 2, rows // LANE_ROWS, LANE_ROWS, cols),
        probe_wave, intensity, positions, tables,
    )
    own = pltpu.with_memory_space_constraint(own, pltpu.VMEM)
    got = pltpu.with_memory_space_constraint(got, pltpu.VMEM)
    acc = pltpu.with_memory_space_constraint(acc, pltpu.VMEM)
    meta = pltpu.with_memory_space_constraint(meta, pltpu.VMEM)
    placed, _ = pl.pallas_call(
        place_kernel,
        out_shape=(
            jax.ShapeDtypeStruct(object_delta.shape, F32),
            pltpu.VMEM(object_delta.shape, F32),
        ),
        in_specs=[vmem, vmem, vmem, vmem],
        out_specs=(anywhere, vmem),
        scratch_shapes=[dma((per, 2, 4))],
        compiler_params=pltpu.CompilerParams(vmem_limit_bytes=56 << 20),
        input_output_aliases={3: 1},
        name="place",
    )(own, got, meta, acc)
    return placed


def solution(mesh):
    def whole(object_delta, probe_wave, intensity, positions):
        tables = jnp.asarray(make_tables(probe_wave.shape[-1]))
        return jax.shard_map(
            per_device,
            mesh=mesh,
            in_specs=(
                P(),
                P("cuts", None, None, "tile"),
                P(),
                P("tile", None, None),
                P("tile", None),
            ),
            out_specs=P("cuts", None, None, "tile"),
            check_vma=False,
        )(tables, object_delta, probe_wave, intensity, positions)

    return whole
```
